32 devices in a mesh: depth: 8 (over z, y), batch: 4 (over x, core).
Axes of the slice: x: 2, y: 2, z: 4, core: 2. Of those that a mesh axis runs over, the one named last changes fastest.
Arguments:
- iterate: float32 [8, 8, 16, 16, 256], P('depth', 'batch'), may hold values from -70 to 70
- weights: bfloat16 [32, 3, 3, 256, 256], P('depth'), may hold values from -0.125 to 0.125
- norm_scale: float32 [32, 256], P('depth'), may hold values from 0.5 to 2
- norm_shift: float32 [32, 256], P('depth'), may hold values from -3 to 3
Outputs:
- block_ends: float32 [8, 8, 16, 16, 256], P('depth', 'batch')
The draws below stay inside these ranges and needn't reach their ends.
All inputs are finite; a program needn't handle non-finite values.
Results may differ from the reference program's by a relative error of at most 0.0018.
Values sent between devices are 32-bit elements; how exact they have to be, the bound alone decides.
No kernel may reach another device: no remote copies, remote signals or barrier semaphores. Data moves between devices by JAX's collectives and lax.ppermute only.
A program may use at most 64 MiB of HBM per device.

```python
import math
import jax
import jax.numpy as jnp
from jax import lax

C = 256
SIDE = 16
SAMPLES = 2
BLOCKS = 8
LAYERS = 32
BATCH = 8


def draw_iterate(key, part):
    key_list = jax.random.split(key, 7)
    array_shape = (BLOCKS, BATCH, SIDE, SIDE, C)
    raw_values = jnp.clip(jax.random.normal(key_list[0], array_shape, jnp.float32), -4.0, 4.0)
    pixel_low = math.log(0.3)
    pixel_scale = jnp.exp(jax.random.uniform(key_list[1], (BLOCKS, BATCH, SIDE, SIDE, 1), jnp.float32, pixel_low, math.log(3.0)))
    channel_scale = jnp.exp(jax.random.uniform(key_list[2], (BLOCKS, 1, 1, 1, C), jnp.float32, math.log(0.3), math.log(3.0)))
    groups = BATCH // SAMPLES
    magnitude = jax.random.uniform(key_list[5], (groups, C), jnp.float32, 2.0, 4.0)
    signs = jnp.where(jax.random.bernoulli(key_list[6], 0.5, (groups, C)), 1.0, -1.0).astype(jnp.float32)
    owner = jnp.arange(BATCH) // SAMPLES
    shifted = (magnitude * signs)[owner].reshape(1, BATCH, 1, 1, C)
    fraction = jnp.arange(BATCH, dtype=jnp.float32) / max(BATCH - 1, 1)
    sample_scale = jnp.exp(math.log(3.0) * (fraction - 0.5)).reshape(1, BATCH, 1, 1, 1)
    return ((raw_values * pixel_scale * channel_scale + shifted) * sample_scale).astype(jnp.float32)


def level_of(rng, dims, shards, smallest, top_value):
    def one(position, parts):
        heights = jax.random.uniform(jax.random.fold_in(jax.random.fold_in(rng, 6), position), (parts,), jnp.float32, smallest / len(shards), top_value / len(shards))
        return jnp.repeat(jnp.exp(heights), dims[position] // parts).reshape((-1,) + (1,) * (len(dims) - position - 1))

    level = one(*shards[0])
    for cut in shards[1:]:
        level = level * one(*cut)
    return level


def scatter_about(stream_key, dims, scale, most, pieces=(), held_as=jnp.bfloat16):
    level = level_of(stream_key, dims, pieces, -0.22, 0.18) if pieces else 1.0
    array = jax.random.normal(stream_key, dims, jnp.float32) * scale * level
    return jnp.minimum(jnp.maximum(array, -most), most).astype(held_as)


def setup_inputs(seed: int = 0) -> dict:
    keys = jax.random.split(jax.random.key(seed), 5)
    iterate = draw_iterate(jax.random.fold_in(keys[4], 71), 0)
    weights = scatter_about(keys[1], (LAYERS, 3, 3, C, C), (9 * C) ** -0.5, 0.125, ((0, 8),))
    norm_scale = jnp.clip(jnp.exp(math.log(2.0) - 1.3862944 * jax.random.uniform(keys[2], (LAYERS, C), jnp.float32) ** level_of(keys[2], (LAYERS, C), ((0, 8),), -0.2, 0.2)), 0.5, 2.0)
    norm_shift = scatter_about(keys[3], (LAYERS, C), 0.5, 3.0, ((0, 8),), jnp.float32)
    return {"iterate": iterate, "weights": weights, "norm_scale": norm_scale, "norm_shift": norm_shift}


fine_step = 0.125
coarse_step = 0.5
epsilon = 1e-05

def convolve(activated, kernel):
    return lax.conv_general_dilated(activated.astype(jnp.float32), kernel.astype(jnp.float32), (1, 1), 'SAME', dimension_numbers=('NHWC', 'HWIO', 'NHWC'), precision=lax.Precision.HIGHEST, preferred_element_type=jnp.float32)

def activate(current, gain_row, offset, center, inverse):
    return jax.nn.relu(gain_row * (current - center) * inverse + offset).astype(jnp.bfloat16)

def fine_layer(current, kernel, gain_row, offset):
    entries = current.shape[0] * current.shape[1] * current.shape[2]
    center = lax.optimization_barrier(jnp.sum(current, axis=(0, 1, 2))) / entries
    inverse = lax.rsqrt(lax.optimization_barrier(jnp.sum(current * current, axis=(0, 1, 2))) / entries - center * center + epsilon)
    activated = activate(current, gain_row, offset, center, inverse)
    return (current + fine_step * convolve(activated, kernel), center, inverse)

def block_map(current, kernels, gains, offsets):
    first_center = None
    first_inverse = None
    for number in range(4):
        current, center, inverse = fine_layer(current, kernels[number], gains[number], offsets[number])
        if number == 0:
            first_center, first_inverse = (center, inverse)
    return (current, first_center, first_inverse)

def reference(iterate, weights, norm_scale, norm_shift):
    kernels = weights.reshape(BLOCKS, 4, 3, 3, C, C)
    gains = norm_scale.reshape(BLOCKS, 4, C)
    offsets = norm_shift.reshape(BLOCKS, 4, C)

    def relax_block(operands):
        return block_map(operands[0], operands[1], operands[2], operands[3])[0]
    relaxed = lax.map(relax_block, (iterate, kernels, gains, offsets))
    begins = jnp.concatenate([iterate[:1], relaxed[:-1]], axis=0)

    def chain_step(carried, operands):
        begin_state, kernel_set, gain_set, offset_set = operands
        fine_end, center, inverse = block_map(begin_state, kernel_set, gain_set, offset_set)

        def coarse(incoming):
            activated = activate(incoming, gain_set[0], offset_set[0], center, inverse)
            return incoming + coarse_step * convolve(activated, kernel_set[0])
        forcing = fine_end - coarse(begin_state)
        produced = coarse(carried) + forcing
        return (produced, produced)
    final_state, block_ends = lax.scan(chain_step, iterate[0], (begins, kernels, gains, offsets))
    return block_ends
```

```python
import functools
import jax
import jax.numpy as jnp
from jax import lax
from jax.experimental import pallas as pl
from jax.experimental.pallas import tpu as pltpu
from jax.sharding import PartitionSpec as P

fine_step = 0.125
coarse_step = 0.5
epsilon = 1e-05
layers_of_block = 4
vmem_bytes = 16 << 20


whole = pl.BlockSpec(memory_space=pltpu.VMEM)
scalars = pl.BlockSpec(memory_space=pltpu.SMEM)


def call(body, operands, outs, scratch=(), specs=None, aliases=None, name=None, flops=0, moved=0):
    return pl.pallas_call(
        body,
        out_shape=outs,
        in_specs=[whole] * len(operands) if specs is None else specs,
        out_specs=jax.tree.map(lambda _: whole, outs),
        scratch_shapes=list(scratch),
        input_output_aliases=aliases or {},
        compiler_params=pltpu.CompilerParams(vmem_limit_bytes=vmem_bytes),
        cost_estimate=pl.CostEstimate(flops=flops, bytes_accessed=moved, transcendentals=0),
        name=name,
    )(*operands)


def f32(*shape):
    return jax.ShapeDtypeStruct(shape, jnp.float32)


def lay_out(activated, taps, width):
    entries, channels = activated.shape
    column = lax.broadcasted_iota(jnp.int32, (entries, 1), 0) % width
    before = jnp.where(column == 0, 0.0, pltpu.roll(activated, 1, 0))
    after = jnp.where(column == width - 1, 0.0, pltpu.roll(activated, entries - 1, 0))
    edge = jnp.zeros((width, 3 * channels), jnp.bfloat16)
    taps[0:width] = edge
    taps[width + entries :] = edge
    for place, values in enumerate((before, activated, after)):
        taps[width : width + entries, place * channels : (place + 1) * channels] = values.astype(
            jnp.bfloat16
        )


def convolved(taps, kernel, width, entries):
    total = jnp.dot(taps[0:entries], kernel(0), preferred_element_type=jnp.float32)
    for row in (1, 2):
        total += jnp.dot(
            taps[row * width : row * width + entries],
            kernel(row),
            preferred_element_type=jnp.float32,
        )
    return total


def both_sums(values):
    return jnp.concatenate(
        [jnp.sum(values, axis=0, keepdims=True), jnp.sum(values * values, axis=0, keepdims=True)],
        axis=0,
    )


def sums_kernel(state, sums):
    samples, rows, width, channels = state.shape
    total = jnp.zeros((2, channels), jnp.float32)
    for i in range(samples):
        total += both_sums(state[i].reshape(rows * width, channels))
    sums[...] = total


def statistics(totals, entries):
    center = totals[0:1] * (1.0 / entries)
    return center, lax.rsqrt(totals[1:2] * (1.0 / entries) - center * center + epsilon)


def layer_kernel(number, parts, batch_entries, kind, *refs):
    state, weights, gains, offsets = refs[:4]
    totals = refs[4 : 4 + parts]
    refs = refs[4 + parts :]
    if kind == "last":
        coarse_begin, first_terms, parity = refs[:3]
        first_outs, taps = refs[3:-1], refs[-1]
    else:
        first_outs, taps = refs[:-1], refs[-1]
    samples, rows, width, channels = state.shape
    entries = rows * width
    summed = totals[0][...]
    for part in totals[1:]:
        summed = summed + part[...]
    center, inverse = statistics(summed, batch_entries)
    scale = gains[number : number + 1] * inverse
    offset = offsets[number : number + 1]
    for i in range(samples):
        values = state[i].reshape(entries, channels)
        lay_out(jnp.maximum((values - center) * scale + offset, 0.0), taps.at[i], width)
    total = jnp.zeros((2, channels), jnp.float32)
    for i in range(samples):
        change = convolved(taps.at[i], lambda row: weights[number, row], width, entries)
        values = state[i].reshape(entries, channels)
        made = values + fine_step * change
        if kind == "last":
            begun = coarse_begin[i].reshape(entries, channels)
            forcing = made - begun
            first_outs[0][i] = (begun + forcing).reshape(rows, width, channels)
            first_outs[1][i] = forcing
        else:
            first_outs[0][i] = made.reshape(rows, width, channels)
            total += both_sums(made)
            if kind == "first":
                first_outs[2][i] = (values + coarse_step * change).reshape(rows, width, channels)
    if kind == "last":
        half = samples // 2
        sent = first_outs[2]
        other = (1 - parity[0]) * half
        for i in range(half):
            sent[i * entries : (i + 1) * entries] = first_outs[1][other + i]
        sent[half * entries :] = first_terms[...]
    else:
        first_outs[1][...] = total
    if kind == "first":
        first_outs[3][...] = jnp.concatenate(
            [center, scale, offset, jnp.zeros((5, channels), jnp.float32)], axis=0
        )


def layer(number, state, weights, gains, offsets, totals, batch_entries, kind, extra=()):
    samples, rows, width, channels = state.shape
    entries = rows * width
    if kind == "last":
        outs = (
            f32(*state.shape),
            f32(samples, entries, channels),
            f32((samples // 2) * entries + 8, channels),
        )
    else:
        outs = (f32(*state.shape), f32(2, channels))
        if kind == "first":
            outs += (f32(*state.shape), f32(8, channels))
    operands = (state, weights, gains, offsets, *totals, *extra)
    specs = [whole] * len(operands)
    if kind == "last":
        specs[-1] = scalars
    return call(
        functools.partial(layer_kernel, number, len(totals), batch_entries, kind),
        operands,
        outs,
        [pltpu.VMEM((samples, entries + 2 * width, 3 * channels), jnp.bfloat16)],
        specs,
        name=f"layer_{kind}",
        flops=2 * samples * entries * 9 * channels * channels,
        moved=4 * samples * entries * channels,
    )


def widen_kernel(core, weights, out):
    half = out.shape[0] // 3
    for row in range(3):
        at = pl.multiple_of(core[0] * half, half)
        out[row * half : (row + 1) * half] = weights[0, row, pl.ds(at, half)].astype(jnp.float32)


def gather_kernel(places, weights, near, far, out):
    parity, core = places[0], places[1]
    half = near.shape[0] // 3
    out[parity] = weights[0]
    other = 1 - parity
    for row in range(3):
        source = slice(row * half, (row + 1) * half)
        here = pl.multiple_of(core * half, half)
        there = pl.multiple_of((1 - core) * half, half)
        out[other, row, pl.ds(here, half)] = near[source].astype(jnp.bfloat16)
        out[other, row, pl.ds(there, half)] = far[source].astype(jnp.bfloat16)


def pair_kernel(turn, inputs, places, *refs):
    arriving = refs[:inputs]
    forcing, exchanged, terms, weights, _, _, first_out, second_out, taps, terms_by, begun = refs[
        inputs:
    ]
    half, rows, width, channels = first_out.shape
    entries = rows * width
    parity = places[0]

    @pl.when(places[2] == turn)
    def _():
        terms_by[parity] = terms[...]
        terms_by[1 - parity] = exchanged[half * entries :]
        for i in range(half):
            begun[parity, i] = forcing[parity * half + i]
            begun[1 - parity, i] = exchanged[i * entries : (i + 1) * entries]
        for i in range(half):
            if inputs == 1:
                values = arriving[0][i].reshape(entries, channels)
            else:
                values = jnp.where(parity == 0, arriving[0][i], arriving[1][i])
                values = values.reshape(entries, channels)
            for stage, out in ((0, first_out), (1, second_out)):
                center, scale, offset = (terms_by[stage, n : n + 1] for n in range(3))
                lay_out(jnp.maximum((values - center) * scale + offset, 0.0), taps, width)
                change = convolved(taps, lambda row: weights[stage, row], width, entries)
                values = values + coarse_step * change + begun[stage, i]
                out[i] = values.reshape(rows, width, channels)


def finish_kernel(places, early, first, second, returned, out):
    half = first.shape[0]
    parity = places[0]

    @pl.when(places[2] == 0)
    def _():
        out[...] = early[...]

    @pl.when(places[2] > 0)
    def _():
        @pl.when(parity == 0)
        def _():
            out[0:half] = first[...]
            out[half:] = returned[...]

        @pl.when(parity == 1)
        def _():
            out[0:half] = returned[...]
            out[half:] = second[...]


def shards(iterate, weights, norm_scale, norm_shift):
    initial = iterate[0]
    samples, rows, width, channels = initial.shape
    half = samples // 2
    position = lax.axis_index("depth")
    place = lax.axis_index("batch")
    devices = lax.axis_size("depth")
    group = lax.axis_size("batch")
    batch_entries = samples * rows * width * group
    parity, core = position % 2, place % 2
    places = jnp.stack([parity, core, position // 2]).astype(jnp.int32)
    weights = weights.reshape(layers_of_block, 3, 3 * channels, channels)

    def gathered(sums):
        routes = [[(i, i ^ m) for i in range(group)] for m in range(1, group)]
        return (sums, *(lax.ppermute(sums, "batch", route) for route in routes))

    partners = [(i, i ^ 1) for i in range(devices)]
    later_partners = [(i, i ^ 1) for i in range(2, devices)]

    sent = call(
        widen_kernel,
        (core.reshape(1).astype(jnp.int32), weights),
        f32(9 * channels // 2, channels),
        specs=[scalars, whole],
        name="widen",
        moved=9 * channels * channels * 3,
    )
    near = lax.ppermute(sent, "depth", partners)

    sums = call(sums_kernel, (initial,), f32(2, channels), name="sums", moved=initial.size * 4)
    first_totals = gathered(sums)
    current, totals = initial, first_totals
    for number in range(layers_of_block):
        current, sums = layer(
            number, current, weights, norm_scale, norm_shift, totals, batch_entries, "plain"
        )
        totals = gathered(sums)
    onward = [(i, i + 1) for i in range(devices - 1)]
    arrived = lax.ppermute(current, "depth", onward)
    arrived_totals = lax.ppermute(sum(totals[1:], totals[0]), "depth", onward)
    begin = jnp.where(position == 0, initial, arrived)
    begin_totals = jnp.where(
        position == 0, sum(first_totals[1:], first_totals[0]), arrived_totals
    )
    far = lax.ppermute(near, "batch", [(i, i ^ 1) for i in range(group)])
    kernels = call(
        gather_kernel,
        (places, weights, near, far),
        jax.ShapeDtypeStruct((2, 3, 3 * channels, channels), jnp.bfloat16),
        specs=[scalars, whole, whole, whole],
        name="gather",
        moved=9 * channels * channels * 8,
    )

    current, sums, coarse_begin, terms = layer(
        0, begin, weights, norm_scale, norm_shift, (begin_totals,), batch_entries, "first"
    )
    for number in range(1, layers_of_block - 1):
        current, sums = layer(
            number, current, weights, norm_scale, norm_shift, gathered(sums), batch_entries, "plain"
        )
    early, forcing, outgoing = layer(
        layers_of_block - 1,
        current,
        weights,
        norm_scale,
        norm_shift,
        gathered(sums),
        batch_entries,
        "last",
        (coarse_begin, terms, places),
    )

    exchanged = lax.ppermute(outgoing, "depth", later_partners)
    arriving = (
        lax.ppermute(early[:half], "depth", [(1, 2)]),
        lax.ppermute(early[half:], "depth", [(1, 3)]),
    )
    shape = (half, rows, width, channels)
    entries = rows * width
    first = jnp.zeros(shape, jnp.float32)
    second = jnp.zeros(shape, jnp.float32)
    for turn in range(1, devices // 2):
        if turn > 1:
            arriving = (
                lax.ppermute(
                    second, "depth", [(2 * turn - 2, 2 * turn), (2 * turn - 1, 2 * turn + 1)]
                ),
            )
        operands = (places, *arriving, forcing, exchanged, terms, kernels, first, second)
        first, second = call(
            functools.partial(pair_kernel, turn, len(arriving)),
            operands,
            (f32(*shape), f32(*shape)),
            [
                pltpu.VMEM((entries + 2 * width, 3 * channels), jnp.bfloat16),
                pltpu.VMEM((2, 8, channels), jnp.float32),
                pltpu.VMEM((2, half, entries, channels), jnp.float32),
            ],
            [scalars] + [whole] * (len(operands) - 1),
            {len(operands) - 2: 0, len(operands) - 1: 1},
            name="pair",
            flops=4 * half * entries * 9 * channels * channels,
            moved=8 * half * entries * channels,
        )
    returned = lax.ppermute(jnp.where(parity == 0, second, first), "depth", later_partners)
    out = call(
        finish_kernel,
        (places, early, first, second, returned),
        f32(*initial.shape),
        specs=[scalars] + [whole] * 4,
        name="finish",
        moved=initial.size * 8,
    )
    return out[None]


def solution(mesh):
    return jax.shard_map(
        shards,
        mesh=mesh,
        in_specs=(
            P("depth", "batch", None, None, None),
            P("depth", None, None, None, None),
            P("depth", None),
            P("depth", None),
        ),
        out_specs=P("depth", "batch", None, None, None),
        check_vma=False,
    )
```

```python
import functools
import jax
import jax.numpy as jnp
from jax import lax
from jax.experimental import pallas as pl
from jax.experimental.pallas import tpu as pltpu
from jax.sharding import PartitionSpec as P

fine_step = 0.125
coarse_step = 0.5
epsilon = 1e-05
layers_of_block = 4
vmem_bytes = 16 << 20


whole = pl.BlockSpec(memory_space=pltpu.VMEM)
in_place = pl.BlockSpec(memory_space=pl.ANY)


def call(
    body, operands, outs, scratch=(), specs=None, out_specs=None, aliases=None, name=None,
    flops=0, moved=0,
):
    return pl.pallas_call(
        body,
        out_shape=outs,
        in_specs=[whole] * len(operands) if specs is None else specs,
        out_specs=jax.tree.map(lambda _: whole, outs) if out_specs is None else out_specs,
        scratch_shapes=list(scratch),
        input_output_aliases=aliases or {},
        compiler_params=pltpu.CompilerParams(vmem_limit_bytes=vmem_bytes),
        cost_estimate=pl.CostEstimate(flops=flops, bytes_accessed=moved, transcendentals=0),
        name=name,
    )(*operands)


def f32(*shape):
    return jax.ShapeDtypeStruct(shape, jnp.float32)


def lay_out(activated, taps, width, above=True, below=True):
    entries, channels = activated.shape
    column = lax.broadcasted_iota(jnp.int32, (entries, 1), 0) % width
    before = jnp.where(column == 0, 0.0, pltpu.roll(activated, 1, 0))
    after = jnp.where(column == width - 1, 0.0, pltpu.roll(activated, entries - 1, 0))
    edge = jnp.zeros((width, 3 * channels), jnp.bfloat16)
    start = width if above else 0
    if above:
        taps[0:width] = edge
    if below:
        taps[start + entries : start + entries + width] = edge
    for place, values in enumerate((before, activated, after)):
        taps[start : start + entries, place * channels : (place + 1) * channels] = values.astype(
            jnp.bfloat16
        )


def convolved(taps, kernel, width, entries):
    total = jnp.dot(taps[0:entries], kernel(0), preferred_element_type=jnp.float32)
    for row in (1, 2):
        total += jnp.dot(
            taps[row * width : row * width + entries],
            kernel(row),
            preferred_element_type=jnp.float32,
        )
    return total


def both_sums(values):
    return jnp.concatenate(
        [jnp.sum(values, axis=0, keepdims=True), jnp.sum(values * values, axis=0, keepdims=True)],
        axis=0,
    )


def sums_kernel(state, sums):
    samples, rows, width, channels = state.shape
    total = jnp.zeros((2, channels), jnp.float32)
    for i in range(samples):
        total += both_sums(state[i].reshape(rows * width, channels))
    sums[...] = total


def statistics(totals, entries):
    center = totals[0:1] * (1.0 / entries)
    return center, lax.rsqrt(totals[1:2] * (1.0 / entries) - center * center + epsilon)


def layer_kernel(number, parts, batch_entries, kind, cut, *refs):
    state, weights, gains, offsets = refs[:4]
    totals = refs[4 : 4 + parts]
    refs = refs[4 + parts :]
    position = lax.axis_index("depth")
    if kind == "first":
        initial, initial_totals = refs[0], refs[1 : 1 + lax.axis_size("batch")]
        outs, taps = refs[1 + len(initial_totals) : -1], refs[-1]
    elif kind == "last":
        coarse_begin, terms = refs[:2]
        outs, taps = refs[2:-1], refs[-1]
    else:
        outs, taps = refs[:-1], refs[-1]
    samples, rows, width, channels = state.shape
    entries = rows * width

    def load(i):
        values = state[i]
        if kind == "first":
            values = jnp.where(position == 0, initial[i], values)
        return values.reshape(entries, channels)

    def added(pieces):
        summed = pieces[0][...]
        for piece in pieces[1:]:
            summed = summed + piece[...]
        return summed

    summed = added(totals)
    if kind == "first":
        summed = jnp.where(position == 0, added(initial_totals), summed)
    center, inverse = statistics(summed, batch_entries)
    scale = gains[number : number + 1] * inverse
    offset = offsets[number : number + 1]
    for i in range(samples):
        lay_out(jnp.maximum((load(i) - center) * scale + offset, 0.0), taps.at[i], width)
    total = jnp.zeros((2, channels), jnp.float32)
    for i in range(samples):
        change = convolved(taps.at[i], lambda row: weights[number, row], width, entries)
        values = load(i)
        made = values + fine_step * change
        if kind == "last":
            begun = coarse_begin[i].reshape(entries, channels)
            forcing = made - begun
            outs[0][i] = (begun + forcing).reshape(rows, width, channels)
            outs[1][i] = forcing
        else:
            outs[0][i] = made.reshape(rows, width, channels)
            total += both_sums(made)
            if kind == "first":
                outs[2][i] = (values + coarse_step * change).reshape(rows, width, channels)
    if kind == "last":
        half = samples // 2
        upper, lower = cut * width, entries - cut * width
        other = (1 - position % 2) * half
        for i in range(half):
            sent = jnp.where(
                position == 1, outs[0][other + i].reshape(entries, channels), outs[1][other + i]
            )
            outs[2][i * upper : (i + 1) * upper] = sent[:upper]
            outs[3][i * lower : (i + 1) * lower] = sent[upper:]
        outs[2][half * upper :] = terms[...]
    else:
        outs[1][...] = total
    if kind == "first":
        outs[3][...] = jnp.concatenate(
            [center, scale, offset, jnp.zeros((5, channels), jnp.float32)], axis=0
        )


def layer(number, state, weights, gains, offsets, totals, batch_entries, kind, extra=(), cut=None):
    samples, rows, width, channels = state.shape
    entries = rows * width
    half = samples // 2
    if kind == "last":
        outs = (
            f32(*state.shape),
            f32(samples, entries, channels),
            f32(half * cut * width + 8, channels),
            f32(half * (rows - cut) * width, channels),
        )
    else:
        outs = (f32(*state.shape), f32(2, channels))
        if kind == "first":
            outs += (f32(*state.shape), f32(8, channels))
    return call(
        functools.partial(layer_kernel, number, len(totals), batch_entries, kind, cut),
        (state, weights, gains, offsets, *totals, *extra),
        outs,
        [pltpu.VMEM((samples, entries + 2 * width, 3 * channels), jnp.bfloat16)],
        name=f"layer_{kind}",
        flops=2 * samples * entries * 9 * channels * channels,
        moved=4 * samples * entries * channels,
    )


def widen_kernel(part, weights, after, out, held, done):
    piece = out.shape[0] // 3
    at = pl.multiple_of((lax.axis_index("batch") % 2) * 2 * piece + part * piece, piece)
    copy = pltpu.make_async_copy(weights.at[0, :, pl.ds(at, piece)], held, done)
    copy.start()
    copy.wait()
    for row in range(3):
        out[row * piece : (row + 1) * piece] = held[row].astype(jnp.float32)


def widen(part, weights, after):
    inner, channels = weights.shape[2:]
    piece = inner // 4
    return call(
        functools.partial(widen_kernel, part),
        (weights, after),
        f32(3 * piece, channels),
        [pltpu.VMEM((3, piece, channels), jnp.bfloat16), pltpu.SemaphoreType.DMA],
        specs=[in_place, whole],
        name="widen",
        moved=3 * piece * channels * 6,
    )


def gather_kernel(weights, near_upper, near_lower, far_upper, far_lower, out):
    parity, core = lax.axis_index("depth") % 2, lax.axis_index("batch") % 2
    piece = near_upper.shape[0] // 3
    out[parity] = weights[0]
    for part, pieces in enumerate(((near_upper, far_upper), (near_lower, far_lower))):
        for owner, source in ((core, pieces[0]), (1 - core, pieces[1])):
            at = pl.multiple_of(owner * 2 * piece + part * piece, piece)
            for row in range(3):
                values = source[row * piece : (row + 1) * piece]
                out[1 - parity, row, pl.ds(at, piece)] = values.astype(jnp.bfloat16)


def relay_kernel(first, received, early, out):
    half, rows, width, channels = out.shape
    entries = rows * width
    odd = lax.axis_index("depth") % 2 == 1
    for i in range(half):
        passed = received[i * entries : (i + 1) * entries].reshape(rows, width, channels)
        out[i] = jnp.where(odd, early[half + i, first : first + rows], passed)


def pair_kernel(turn, mode, cut, exchange_cut, kept_cut, out_cut, *refs):
    incoming = refs[: 1 if mode == "upper" else 2]
    refs = refs[len(incoming) :]
    if mode == "lower":
        first_upper, refs = refs[0], refs[1:]
    forcing, upper_exchange, lower_exchange, terms, kernels = refs[:5]
    refs = refs[5 + 3 :]
    made, own, give_upper, give_lower, taps = refs[:-4], refs[-4], refs[-3], refs[-2], refs[-1]
    samples = forcing.shape[0]
    half, height, width, channels = own.shape
    position = lax.axis_index("depth")
    parity = position % 2

    def flat(values):
        return values.reshape(-1, channels)

    def forced(stage, i, low, high):
        here = forcing[parity * half + i, low * width : high * width]
        there = []
        if low < exchange_cut:
            base = i * exchange_cut
            last = min(high, exchange_cut)
            there.append(upper_exchange[(base + low) * width : (base + last) * width])
        if high > exchange_cut:
            base = i * (height - exchange_cut) - exchange_cut
            there.append(
                lower_exchange[(base + max(low, exchange_cut)) * width : (base + high) * width]
            )
        there = there[0] if len(there) == 1 else jnp.concatenate(there, axis=0)
        return jnp.where(parity == stage, here, there)

    def mapped(stage, i, values, begin, low, high):
        base = half * exchange_cut * width
        center, scale, offset = (
            jnp.where(parity == stage, terms[n : n + 1], upper_exchange[base + n : base + n + 1])
            for n in range(3)
        )
        lay_out(
            jnp.maximum((values - center) * scale + offset, 0.0),
            taps.at[i, stage],
            width,
            low == 0,
            high == height,
        )
        change = convolved(
            taps.at[i, stage], lambda row: kernels[stage, row], width, (high - low) * width
        )
        kept = values[(low - begin) * width : (high - begin) * width]
        return kept + coarse_step * change + forced(stage, i, low, high)

    def put(i, low, values, is_own):
        high = low + values.shape[0] // width
        values = values.reshape(high - low, width, channels)
        if is_own:
            own[i, low:high] = values
            return
        if low < kept_cut:
            last = min(high, kept_cut)
            give_upper[i, low:last] = values[: last - low]
        if high > kept_cut:
            first = max(low, kept_cut)
            give_lower[i, first - kept_cut : high - kept_cut] = values[first - low :]

    @pl.when(position // 2 == turn)
    def _():
        for i in range(half):
            if mode == "upper":
                low = 0
                first = mapped(0, i, flat(incoming[0][i]), 0, 0, cut - 1)
                second = mapped(1, i, first, 0, 0, cut - 2)
                first_low, second_low = 0, 0
                made[0][i] = first.reshape(-1, width, channels)
                made[1][i] = second.reshape(-1, width, channels)
            elif mode == "lower":
                first_low, second_low = cut - 1, cut - 2
                values = jnp.concatenate(
                    [flat(incoming[0][i, cut - 2 :]), flat(incoming[1][i])], axis=0
                )
                first = mapped(0, i, values, cut - 2, cut - 1, height)
                values = jnp.concatenate([flat(first_upper[i, cut - 3 :]), first], axis=0)
                second = mapped(1, i, values, cut - 3, cut - 2, height)
                made[0][i] = second.reshape(-1, width, channels)
            else:
                first_low, second_low = 0, 0
                values = jnp.concatenate([flat(incoming[0][i]), flat(incoming[1][i])], axis=0)
                first = mapped(0, i, values, 0, 0, height)
                second = mapped(1, i, first, 0, 0, height)
                made[0][i] = second[: out_cut * width].reshape(-1, width, channels)
                made[1][i] = second[out_cut * width :].reshape(-1, width, channels)

            @pl.when(parity == 0)
            def _():
                put(i, first_low, first, True)
                put(i, second_low, second, False)

            @pl.when(parity == 1)
            def _():
                put(i, first_low, first, False)
                put(i, second_low, second, True)


def pair(turn, mode, cut, exchange_cut, kept_cut, out_cut, incoming, shared, kept):
    own = kept[0]
    half, height, width, channels = own.shape
    if mode == "upper":
        made = (f32(half, cut - 1, width, channels), f32(half, cut - 2, width, channels))
    elif mode == "lower":
        made = (f32(half, height - cut + 2, width, channels),)
    else:
        made = (f32(half, out_cut, width, channels), f32(half, height - out_cut, width, channels))
    operands = (*incoming, *shared, *kept)
    count = len(operands) - len(kept)
    entries = half * height * width
    outs = call(
        functools.partial(pair_kernel, turn, mode, cut, exchange_cut, kept_cut, out_cut),
        operands,
        made + tuple(f32(*piece.shape) for piece in kept),
        [pltpu.VMEM((half, 2, (height + 2) * width, 3 * channels), jnp.bfloat16)],
        aliases={count + n: len(made) + n for n in range(len(kept))},
        name=f"pair_{mode}",
        flops=2 * entries * 9 * channels * channels,
        moved=4 * entries * channels,
    )
    return outs[: len(made)], outs[len(made) :]


def finish_own_kernel(early, own, out, done):
    half = own.shape[0]
    position = lax.axis_index("depth")

    @pl.when(position < 2)
    def _():
        copy = pltpu.make_async_copy(early, out, done)
        copy.start()
        copy.wait()

    @pl.when(position >= 2)
    def _():
        copy = pltpu.make_async_copy(own, out.at[pl.ds((position % 2) * half, half)], done)
        copy.start()
        copy.wait()


def finish_kernel(upper, lower, _, out, upper_done, lower_done):
    half, cut = upper.shape[:2]
    position = lax.axis_index("depth")

    @pl.when(position >= 2)
    def _():
        there = pl.ds((1 - position % 2) * half, half)
        first = pltpu.make_async_copy(upper, out.at[there, 0:cut], upper_done)
        second = pltpu.make_async_copy(lower, out.at[there, cut : out.shape[1]], lower_done)
        first.start()
        second.start()
        first.wait()
        second.wait()


def turns_of(count, height):
    start = height * 11 // 16
    plan, cut = [], start
    for _ in range(count):
        split = cut >= 4
        plan.append((cut, split, cut - 2 if split else start))
        cut = plan[-1][2]
    return start, plan


def shards(iterate, weights, norm_scale, norm_shift):
    initial = iterate[0]
    samples, rows, width, channels = initial.shape
    half = samples // 2
    devices = lax.axis_size("depth")
    group = lax.axis_size("batch")
    batch_entries = samples * rows * width * group
    weights = weights.reshape(layers_of_block, 3, 3 * channels, channels)
    run = functools.partial(layer, batch_entries=batch_entries)
    norms = (weights, norm_scale, norm_shift)

    def gathered(sums):
        routes = [[(i, i ^ m) for i in range(group)] for m in range(1, group)]
        return (sums, *(lax.ppermute(sums, "batch", route) for route in routes))

    partners = [(i, i ^ 1) for i in range(devices)]
    cores = [(i, i ^ 1) for i in range(group)]
    onward = [(i, i + 1) for i in range(devices - 1)]

    sums = call(sums_kernel, (initial,), f32(2, channels), name="sums", moved=initial.size * 4)
    first_totals = gathered(sums)
    current, totals = initial, first_totals
    for number in range(layers_of_block):
        current, sums = run(number, current, *norms, totals, kind="plain")
        if number == 0:
            near_upper = lax.ppermute(widen(0, weights, sums), "depth", partners)
        totals = gathered(sums)
    arrived = lax.ppermute(current, "depth", onward)
    arrived_totals = lax.ppermute(sum(totals[1:], totals[0]), "depth", onward)

    start, plan = turns_of(devices // 2 - 1, rows)
    current, sums, coarse_begin, terms = run(
        0, arrived, *norms, (arrived_totals,), kind="first", extra=(initial, *first_totals)
    )
    near_lower = lax.ppermute(widen(1, weights, sums), "depth", partners)
    far_upper = lax.ppermute(near_upper, "batch", cores)
    for number in range(1, layers_of_block - 1):
        current, sums = run(number, current, *norms, gathered(sums), kind="plain")
    far_lower = lax.ppermute(near_lower, "batch", cores)
    early, forcing, upper_sent, lower_sent = run(
        layers_of_block - 1,
        current,
        *norms,
        gathered(sums),
        kind="last",
        extra=(coarse_begin, terms),
        cut=start,
    )
    kernels = call(
        gather_kernel,
        (weights, near_upper, near_lower, far_upper, far_lower),
        jax.ShapeDtypeStruct((2, 3, 3 * channels, channels), jnp.bfloat16),
        name="gather",
        moved=9 * channels * channels * 8,
    )

    swaps = [pair for pair in partners if pair != (0, 1)]
    upper_exchange = lax.ppermute(upper_sent, "depth", swaps)
    lower_exchange = lax.ppermute(lower_sent, "depth", swaps)
    passed = []
    for first, received, height in (
        (0, upper_exchange, start),
        (start, lower_exchange, rows - start),
    ):
        passed.append(
            call(
                functools.partial(relay_kernel, first),
                (received, early),
                f32(half, height, width, channels),
                name="relay",
                moved=half * height * width * channels * 8,
            )
        )
    kept_cut = plan[-1][2]
    own = jnp.zeros((half, rows, width, channels), jnp.float32)
    give_upper = jnp.zeros((half, kept_cut, width, channels), jnp.float32)
    give_lower = jnp.zeros((half, rows - kept_cut, width, channels), jnp.float32)
    shared = (forcing, upper_exchange, lower_exchange, terms, kernels)
    for turn, (cut, split, out_cut) in enumerate(plan, 1):
        route = [(2 * turn - 2, 2 * turn), (2 * turn - 1, 2 * turn + 1)]
        arriving = [lax.ppermute(piece, "depth", route) for piece in passed]
        cuts = (cut, start, kept_cut, out_cut)
        if split:
            (first, second), kept = pair(
                turn, "upper", *cuts, arriving[:1], shared, (own, give_upper, give_lower)
            )
            own, give_upper, give_lower = kept
            passed = [second]
            if turn == len(plan):
                returned_upper = lax.ppermute(give_upper, "depth", partners[2:])
                give_upper = jnp.zeros_like(give_upper)
            (second,), kept = pair(
                turn, "lower", *cuts, (*arriving, first), shared, (own, give_upper, give_lower)
            )
            passed.append(second)
        else:
            passed, kept = pair(
                turn, "full", *cuts, arriving, shared, (own, give_upper, give_lower)
            )
        own, give_upper, give_lower = kept
    if not plan[-1][1]:
        returned_upper = lax.ppermute(give_upper, "depth", partners[2:])
    returned_lower = lax.ppermute(give_lower, "depth", partners[2:])
    out = call(
        finish_own_kernel,
        (early, own),
        f32(*initial.shape),
        [pltpu.SemaphoreType.DMA],
        out_specs=in_place,
        name="finish_own",
        moved=initial.size * 8,
    )
    out = call(
        finish_kernel,
        (returned_upper, returned_lower, out),
        f32(*initial.shape),
        [pltpu.SemaphoreType.DMA, pltpu.SemaphoreType.DMA],
        specs=[whole, whole, in_place],
        out_specs=in_place,
        aliases={2: 0},
        name="finish",
        moved=initial.size * 4,
    )
    return out[None]


def solution(mesh):
    return jax.shard_map(
        shards,
        mesh=mesh,
        in_specs=(
            P("depth", "batch", None, None, None),
            P("depth", None, None, None, None),
            P("depth", None),
            P("depth", None),
        ),
        out_specs=P("depth", "batch", None, None, None),
        check_vma=False,
    )
```

```python
import functools
import jax
import jax.numpy as jnp
from jax import lax
from jax.experimental import pallas as pl
from jax.experimental.pallas import tpu as pltpu
from jax.sharding import PartitionSpec as P

fine_step = 0.125
coarse_step = 0.5
epsilon = 1e-05
layers_of_block = 4
vmem_bytes = 16 << 20


whole = pl.BlockSpec(memory_space=pltpu.VMEM)
in_place = pl.BlockSpec(memory_space=pltpu.HBM)


def call(
    body, operands, outs, scratch=(), specs=None, out_specs=None, aliases=None,
    flops=0, moved=0,
):
    return pl.pallas_call(
        body,
        out_shape=outs,
        in_specs=[whole] * len(operands) if specs is None else specs,
        out_specs=jax.tree.map(lambda _: whole, outs) if out_specs is None else out_specs,
        scratch_shapes=list(scratch),
        input_output_aliases=aliases or {},
        compiler_params=pltpu.CompilerParams(vmem_limit_bytes=vmem_bytes),
        cost_estimate=pl.CostEstimate(flops=flops, bytes_accessed=moved, transcendentals=0),
    )(*operands)


def f32(*shape):
    return jax.ShapeDtypeStruct(shape, jnp.float32)


def lay_out(activated, taps, width, above=True, below=True):
    entries, channels = activated.shape
    column = lax.broadcasted_iota(jnp.int32, (entries, 1), 0) % width
    before = jnp.where(column == 0, 0.0, pltpu.roll(activated, 1, 0))
    after = jnp.where(column == width - 1, 0.0, pltpu.roll(activated, entries - 1, 0))
    edge = jnp.zeros((width, 3 * channels), jnp.bfloat16)
    start = width if above else 0
    if above:
        taps[0:width] = edge
    if below:
        taps[start + entries : start + entries + width] = edge
    for place, values in enumerate((before, activated, after)):
        taps[start : start + entries, place * channels : (place + 1) * channels] = values.astype(
            jnp.bfloat16
        )


def convolved(taps, kernel, width, entries):
    total = jnp.dot(taps[0:entries], kernel(0), preferred_element_type=jnp.float32)
    for row in (1, 2):
        total += jnp.dot(
            taps[row * width : row * width + entries],
            kernel(row),
            preferred_element_type=jnp.float32,
        )
    return total


def both_sums(values):
    return jnp.concatenate(
        [jnp.sum(values, axis=0, keepdims=True), jnp.sum(values * values, axis=0, keepdims=True)],
        axis=0,
    )


def sums_kernel(state, sums):
    samples, rows, width, channels = state.shape
    total = jnp.zeros((2, channels), jnp.float32)
    for i in range(samples):
        total += both_sums(state[i].reshape(rows * width, channels))
    sums[...] = total


def copy_kernel(source, out):
    out[...] = source[...]


def statistics(totals, entries):
    center = totals[0:1] * (1.0 / entries)
    return center, lax.rsqrt(totals[1:2] * (1.0 / entries) - center * center + epsilon)


def layer_kernel(number, parts, batch_entries, kind, cut, *refs):
    state, weights, gains, offsets = refs[:4]
    totals = refs[4 : 4 + parts]
    refs = refs[4 + parts :]
    position = lax.axis_index("depth")
    if kind == "first":
        initial, initial_totals = refs[0], refs[1 : 1 + lax.axis_size("batch")]
        outs, taps = refs[1 + len(initial_totals) : -1], refs[-1]
    elif kind == "last":
        coarse_begin, terms = refs[:2]
        outs, taps = refs[2:-1], refs[-1]
    else:
        outs, taps = refs[:-1], refs[-1]
    samples, rows, width, channels = state.shape
    entries = rows * width

    def load(i):
        values = state[i]
        if kind == "first":
            values = jnp.where(position == 0, initial[i], values)
        return values.reshape(entries, channels)

    def added(pieces):
        summed = pieces[0][...]
        for piece in pieces[1:]:
            summed = summed + piece[...]
        return summed

    summed = added(totals)
    if kind == "first":
        summed = jnp.where(position == 0, added(initial_totals), summed)
    center, inverse = statistics(summed, batch_entries)
    scale = gains[number : number + 1] * inverse
    offset = offsets[number : number + 1]
    for i in range(samples):
        lay_out(jnp.maximum((load(i) - center) * scale + offset, 0.0), taps.at[i], width)
    total = jnp.zeros((2, channels), jnp.float32)
    for i in range(samples):
        change = convolved(taps.at[i], lambda row: weights[number, row], width, entries)
        values = load(i)
        made = values + fine_step * change
        if kind == "last":
            begun = coarse_begin[i].reshape(entries, channels)
            forcing = made - begun
            ended = (begun + forcing).reshape(rows, width, channels)
            outs[0][i] = ended
            outs[1][i] = forcing
            which, at = divmod(i, samples // 2)
            outs[4 + 2 * which][at] = ended[:cut]
            outs[5 + 2 * which][at] = ended[cut:]
        else:
            outs[0][i] = made.reshape(rows, width, channels)
            total += both_sums(made)
            if kind == "first":
                outs[2][i] = (values + coarse_step * change).reshape(rows, width, channels)
    if kind == "last":
        half = samples // 2
        upper, lower = cut * width, entries - cut * width
        other = (1 - position % 2) * half
        for i in range(half):
            sent = outs[1][other + i]
            outs[2][i * upper : (i + 1) * upper] = sent[:upper]
            outs[3][i * lower : (i + 1) * lower] = sent[upper:]
        outs[2][half * upper :] = terms[...]
    else:
        outs[1][...] = total
    if kind == "first":
        outs[3][...] = jnp.concatenate(
            [center, scale, offset, jnp.zeros((5, channels), jnp.float32)], axis=0
        )


def layer(number, state, weights, gains, offsets, totals, batch_entries, kind, extra=(), cut=None):
    samples, rows, width, channels = state.shape
    entries = rows * width
    half = samples // 2
    if kind == "last":
        outs = (
            f32(*state.shape),
            f32(samples, entries, channels),
            f32(half * cut * width + 8, channels),
            f32(half * (rows - cut) * width, channels),
        ) + 2 * (f32(half, cut, width, channels), f32(half, rows - cut, width, channels))
    else:
        outs = (f32(*state.shape), f32(2, channels))
        if kind == "first":
            outs += (f32(*state.shape), f32(8, channels))
    return call(
        functools.partial(layer_kernel, number, len(totals), batch_entries, kind, cut),
        (state, weights, gains, offsets, *totals, *extra),
        outs,
        [pltpu.VMEM((samples, entries + 2 * width, 3 * channels), jnp.bfloat16)],
        flops=2 * samples * entries * 9 * channels * channels,
        moved=4 * samples * entries * channels,
    )


def widen_kernel(part, weights, after, out, held, done):
    piece = out.shape[0] // 3
    at = pl.multiple_of((lax.axis_index("batch") % 2) * 2 * piece + part * piece, piece)
    copy = pltpu.make_async_copy(weights.at[0, :, pl.ds(at, piece)], held, done)
    copy.start()
    copy.wait()
    for row in range(3):
        out[row * piece : (row + 1) * piece] = held[row].astype(jnp.float32)


def widen(part, weights, after):
    inner, channels = weights.shape[2:]
    piece = inner // 4
    return call(
        functools.partial(widen_kernel, part),
        (weights, after),
        f32(3 * piece, channels),
        [pltpu.VMEM((3, piece, channels), jnp.bfloat16), pltpu.SemaphoreType.DMA],
        specs=[in_place, whole],
        moved=3 * piece * channels * 6,
    )


def gather_kernel(weights, near_upper, near_lower, far_upper, far_lower, out):
    parity, core = lax.axis_index("depth") % 2, lax.axis_index("batch") % 2
    piece = near_upper.shape[0] // 3
    out[parity] = weights[0]
    for part, pieces in enumerate(((near_upper, far_upper), (near_lower, far_lower))):
        for owner, source in ((core, pieces[0]), (1 - core, pieces[1])):
            at = pl.multiple_of(owner * 2 * piece + part * piece, piece)
            for row in range(3):
                values = source[row * piece : (row + 1) * piece]
                out[1 - parity, row, pl.ds(at, piece)] = values.astype(jnp.bfloat16)


def stage_kernel(weights, out, done):
    copies = [
        pltpu.make_async_copy(weights.at[n], out.at[n], done.at[n]) for n in range(out.shape[0])
    ]
    for copy in copies:
        copy.start()
    for copy in copies:
        copy.wait()


def pair_kernel(turn, mode, ways, cut, exchange_cut, kept_cut, out_cut, *refs):
    pieces = 1 if mode == "upper" else 2
    incoming = [refs[n * ways : (n + 1) * ways] for n in range(pieces)]
    refs = refs[pieces * ways :]
    if mode == "lower":
        first_upper, refs = refs[0], refs[1:]
    forcing, upper_exchange, lower_exchange, terms, kernels = refs[:5]
    refs = refs[5 + 3 :]
    made, own, give_upper, give_lower, taps = refs[:-4], refs[-4], refs[-3], refs[-2], refs[-1]
    half, height, width, channels = own.shape
    position = lax.axis_index("depth")
    parity = position % 2

    def flat(values):
        return values.reshape(-1, channels)

    def arrived(piece, i, low=0):
        values = [flat(way[i, low:]) for way in incoming[piece]]
        return values[0] if ways == 1 else jnp.where(parity == 0, values[0], values[1])

    def forced(stage, i, low, high):
        here = forcing[parity * half + i, low * width : high * width]
        there = []
        if low < exchange_cut:
            base = i * exchange_cut
            last = min(high, exchange_cut)
            there.append(upper_exchange[(base + low) * width : (base + last) * width])
        if high > exchange_cut:
            base = i * (height - exchange_cut) - exchange_cut
            there.append(
                lower_exchange[(base + max(low, exchange_cut)) * width : (base + high) * width]
            )
        there = there[0] if len(there) == 1 else jnp.concatenate(there, axis=0)
        return jnp.where(parity == stage, here, there)

    def mapped(stage, i, values, begin, low, high):
        base = half * exchange_cut * width
        center, scale, offset = (
            jnp.where(parity == stage, terms[n : n + 1], upper_exchange[base + n : base + n + 1])
            for n in range(3)
        )
        lay_out(
            jnp.maximum((values - center) * scale + offset, 0.0),
            taps.at[i, stage],
            width,
            low == 0,
            high == height,
        )
        change = convolved(
            taps.at[i, stage], lambda row: kernels[stage, row], width, (high - low) * width
        )
        kept = values[(low - begin) * width : (high - begin) * width]
        return kept + coarse_step * change + forced(stage, i, low, high)

    def put(i, low, values, is_own):
        high = low + values.shape[0] // width
        values = values.reshape(high - low, width, channels)
        if is_own:
            own[i, low:high] = values
            return
        if low < kept_cut:
            last = min(high, kept_cut)
            give_upper[i, low:last] = values[: last - low]
        if high > kept_cut:
            first = max(low, kept_cut)
            give_lower[i, first - kept_cut : high - kept_cut] = values[first - low :]

    @pl.when(position // 2 == turn)
    def _():
        for i in range(half):
            if mode == "upper":
                first = mapped(0, i, arrived(0, i), 0, 0, cut - 1)
                second = mapped(1, i, first, 0, 0, cut - 2)
                first_low, second_low = 0, 0
                made[0][i] = first.reshape(-1, width, channels)
                if len(made) > 1:
                    made[1][i] = second.reshape(-1, width, channels)
            elif mode == "lower":
                first_low, second_low = cut - 1, cut - 2
                values = jnp.concatenate([arrived(0, i, cut - 2), arrived(1, i)], axis=0)
                first = mapped(0, i, values, cut - 2, cut - 1, height)
                values = jnp.concatenate([flat(first_upper[i, cut - 3 :]), first], axis=0)
                second = mapped(1, i, values, cut - 3, cut - 2, height)
                if made:
                    made[0][i] = second.reshape(-1, width, channels)
            else:
                first_low, second_low = 0, 0
                values = jnp.concatenate([arrived(0, i), arrived(1, i)], axis=0)
                first = mapped(0, i, values, 0, 0, height)
                second = mapped(1, i, first, 0, 0, height)
                if made:
                    made[0][i] = second[: out_cut * width].reshape(-1, width, channels)
                    made[1][i] = second[out_cut * width :].reshape(-1, width, channels)

            @pl.when(parity == 0)
            def _():
                put(i, first_low, first, True)
                put(i, second_low, second, False)

            @pl.when(parity == 1)
            def _():
                put(i, first_low, first, False)
                put(i, second_low, second, True)


def pair(turn, mode, cut, exchange_cut, kept_cut, out_cut, incoming, shared, kept, last, extra=()):
    own = kept[0]
    half, height, width, channels = own.shape
    if mode == "upper":
        made = (f32(half, cut - 1, width, channels), f32(half, cut - 2, width, channels))
    elif mode == "lower":
        made = (f32(half, height - cut + 2, width, channels),)
    else:
        made = (f32(half, out_cut, width, channels), f32(half, height - out_cut, width, channels))
    if last:
        made = made[:1] if mode == "upper" else ()
    ways = len(incoming[0])
    operands = (*(way for piece in incoming for way in piece), *extra, *shared, *kept)
    count = len(operands) - len(kept)
    entries = half * height * width
    outs = call(
        functools.partial(pair_kernel, turn, mode, ways, cut, exchange_cut, kept_cut, out_cut),
        operands,
        made + tuple(f32(*piece.shape) for piece in kept),
        [pltpu.VMEM((half, 2, (height + 2) * width, 3 * channels), jnp.bfloat16)],
        aliases={count + n: len(made) + n for n in range(len(kept))},
        flops=2 * entries * 9 * channels * channels,
        moved=4 * entries * channels,
    )
    return outs[: len(made)], outs[len(made) :]


def finish_own_kernel(early, own, out, done):
    half = own.shape[0]
    position = lax.axis_index("depth")

    @pl.when(position < 2)
    def _():
        copy = pltpu.make_async_copy(early, out, done)
        copy.start()
        copy.wait()

    @pl.when(position >= 2)
    def _():
        copy = pltpu.make_async_copy(own, out.at[pl.ds((position % 2) * half, half)], done)
        copy.start()
        copy.wait()


def finish_kernel(upper, lower, _, out, upper_done, lower_done):
    half, cut = upper.shape[:2]
    position = lax.axis_index("depth")

    @pl.when(position >= 2)
    def _():
        there = pl.ds((1 - position % 2) * half, half)
        first = pltpu.make_async_copy(upper, out.at[there, 0:cut], upper_done)
        second = pltpu.make_async_copy(lower, out.at[there, cut : out.shape[1]], lower_done)
        first.start()
        second.start()
        first.wait()
        second.wait()


def turns_of(count, height):
    start = height * 11 // 16
    plan, cut = [], start
    for _ in range(count):
        split = cut >= 4
        plan.append((cut, split, cut - 2 if split else start))
        cut = plan[-1][2]
    return start, plan


def steps(iterate, weights, norm_scale, norm_shift):
    initial = iterate[0]
    samples, rows, width, channels = initial.shape
    half = samples // 2
    devices = lax.axis_size("depth")
    group = lax.axis_size("batch")
    batch_entries = samples * rows * width * group
    stored = weights.reshape(layers_of_block, 3, 3 * channels, channels)
    run = functools.partial(layer, batch_entries=batch_entries)

    def gathered(sums, mark=False):
        others = [
            lax.ppermute(sums, "batch", [(i, i ^ m) for i in range(group)])
            for m in range(1, group)
        ]
        if mark:
            sums = call(copy_kernel, (sums,), f32(*sums.shape))
        return (sums, *others)

    partners = [(i, i ^ 1) for i in range(devices)]
    cores = [(i, i ^ 1) for i in range(group)]
    onward = [(i, i + 1) for i in range(devices - 1)]

    sums = call(sums_kernel, (initial,), f32(2, channels), moved=initial.size * 4)
    first_totals = gathered(sums)
    weights = call(
        stage_kernel,
        (stored,),
        jax.ShapeDtypeStruct(stored.shape, stored.dtype),
        [pltpu.SemaphoreType.DMA((layers_of_block,))],
        specs=[in_place],
        moved=stored.size * 4,
    )
    norms = (weights, norm_scale, norm_shift)
    current, totals = initial, first_totals
    for number in range(layers_of_block):
        current, sums = run(number, current, *norms, totals, kind="plain")
        if number == 0:
            near_upper = lax.ppermute(widen(0, stored, sums), "depth", partners)
        totals = gathered(sums, number == 0)
    arrived = lax.ppermute(current, "depth", onward)
    arrived_totals = lax.ppermute(sum(totals[1:], totals[0]), "depth", onward)

    start, plan = turns_of(devices // 2 - 1, rows)
    current, sums, coarse_begin, terms = run(
        0, arrived, *norms, (arrived_totals,), kind="first", extra=(initial, *first_totals)
    )
    near_lower = lax.ppermute(widen(1, stored, sums), "depth", partners)
    far_upper = lax.ppermute(near_upper, "batch", cores)
    for number in range(1, layers_of_block - 1):
        totals = gathered(sums, number == 1)
        current, sums = run(number, current, *norms, totals, kind="plain")
    far_lower = lax.ppermute(near_lower, "batch", cores)
    early, forcing, upper_sent, lower_sent, *pieces = run(
        layers_of_block - 1,
        current,
        *norms,
        gathered(sums, True),
        kind="last",
        extra=(coarse_begin, terms),
        cut=start,
    )
    kernels = call(
        gather_kernel,
        (weights, near_upper, near_lower, far_upper, far_lower),
        jax.ShapeDtypeStruct((2, 3, 3 * channels, channels), jnp.bfloat16),
        moved=9 * channels * channels * 8,
    )

    upper_exchange = lax.ppermute(upper_sent, "depth", partners[2:])
    lower_exchange = lax.ppermute(lower_sent, "depth", partners[2:])
    kept_cut = plan[-1][2]
    own = jnp.zeros((half, rows, width, channels), jnp.float32)
    give_upper = jnp.zeros((half, kept_cut, width, channels), jnp.float32)
    give_lower = jnp.zeros((half, rows - kept_cut, width, channels), jnp.float32)
    shared = (forcing, upper_exchange, lower_exchange, terms, kernels)
    arriving = [
        [lax.ppermute(pieces[2 * way + part], "depth", [(1, 2 + way)]) for way in (0, 1)]
        for part in (0, 1)
    ]
    for turn, (cut, split, out_cut) in enumerate(plan, 1):
        if turn > 1:
            route = [(2 * turn - 2, 2 * turn), (2 * turn - 1, 2 * turn + 1)]
            arriving = [[lax.ppermute(piece, "depth", route)] for piece in passed]
        cuts = (cut, start, kept_cut, out_cut)
        last = turn == len(plan)
        if split:
            (first, *passed), kept = pair(
                turn, "upper", *cuts, arriving[:1], shared, (own, give_upper, give_lower), last
            )
            own, give_upper, give_lower = kept
            if last:
                returned_upper = lax.ppermute(give_upper, "depth", partners[2:])
                give_upper = jnp.zeros_like(give_upper)
            others, kept = pair(
                turn,
                "lower",
                *cuts,
                arriving,
                shared,
                (own, give_upper, give_lower),
                last,
                (first,),
            )
            passed.extend(others)
        else:
            passed, kept = pair(
                turn, "full", *cuts, arriving, shared, (own, give_upper, give_lower), last
            )
        own, give_upper, give_lower = kept
    if not plan[-1][1]:
        returned_upper = lax.ppermute(give_upper, "depth", partners[2:])
    returned_lower = lax.ppermute(give_lower, "depth", partners[2:])
    out = call(
        finish_own_kernel,
        (early, own),
        f32(*initial.shape),
        [pltpu.SemaphoreType.DMA],
        out_specs=in_place,
        moved=initial.size * 8,
    )
    out = call(
        finish_kernel,
        (returned_upper, returned_lower, out),
        f32(*initial.shape),
        [pltpu.SemaphoreType.DMA, pltpu.SemaphoreType.DMA],
        specs=[whole, whole, in_place],
        out_specs=in_place,
        aliases={2: 0},
        moved=initial.size * 4,
    )
    return out[None]


def solution(mesh):
    return jax.shard_map(
        steps,
        mesh=mesh,
        in_specs=(
            P("depth", "batch", None, None, None),
            P("depth", None, None, None, None),
            P("depth", None),
            P("depth", None),
        ),
        out_specs=P("depth", "batch", None, None, None),
        check_vma=False,
    )
```

```python
import functools
import jax
import jax.numpy as jnp
from jax import lax
from jax.experimental import pallas as pl
from jax.experimental.pallas import tpu as pltpu
from jax.sharding import PartitionSpec as P

fine_step = 0.125
coarse_step = 0.5
epsilon = 1e-05
layers_of_block = 4
vmem_bytes = 16 << 20


whole = pl.BlockSpec(memory_space=pltpu.VMEM)
in_place = pl.BlockSpec(memory_space=pltpu.HBM)


def call(
    body, operands, outs, scratch=(), specs=None, out_specs=None, aliases=None,
    flops=0, moved=0,
):
    return pl.pallas_call(
        body,
        out_shape=outs,
        in_specs=[whole] * len(operands) if specs is None else specs,
        out_specs=jax.tree.map(lambda _: whole, outs) if out_specs is None else out_specs,
        scratch_shapes=list(scratch),
        input_output_aliases=aliases or {},
        compiler_params=pltpu.CompilerParams(vmem_limit_bytes=vmem_bytes),
        cost_estimate=pl.CostEstimate(flops=flops, bytes_accessed=moved, transcendentals=0),
    )(*operands)


def f32(*shape):
    return jax.ShapeDtypeStruct(shape, jnp.float32)


def lay_out(activated, taps, width, above=True, below=True):
    entries, channels = activated.shape
    column = lax.broadcasted_iota(jnp.int32, (entries, 1), 0) % width
    before = jnp.where(column == 0, 0.0, pltpu.roll(activated, 1, 0))
    after = jnp.where(column == width - 1, 0.0, pltpu.roll(activated, entries - 1, 0))
    edge = jnp.zeros((width, 3 * channels), jnp.bfloat16)
    start = width if above else 0
    if above:
        taps[0:width] = edge
    if below:
        taps[start + entries : start + entries + width] = edge
    for place, values in enumerate((before, activated, after)):
        taps[start : start + entries, place * channels : (place + 1) * channels] = values.astype(
            jnp.bfloat16
        )


def convolved(taps, kernel, width, entries):
    total = jnp.dot(taps[0:entries], kernel(0), preferred_element_type=jnp.float32)
    for row in (1, 2):
        total += jnp.dot(
            taps[row * width : row * width + entries],
            kernel(row),
            preferred_element_type=jnp.float32,
        )
    return total


def both_sums(values):
    return jnp.concatenate(
        [jnp.sum(values, axis=0, keepdims=True), jnp.sum(values * values, axis=0, keepdims=True)],
        axis=0,
    )


def spans(cuts, rows):
    edges = (0, *cuts, rows)
    return list(zip(edges, edges[1:]))


def sums_kernel(state, sums):
    samples, rows, width, channels = state.shape
    total = jnp.zeros((2, channels), jnp.float32)
    for i in range(samples):
        total += both_sums(state[i].reshape(rows * width, channels))
    sums[...] = total


def copy_kernel(*refs):
    refs[-1][...] = refs[0][...]


def statistics(totals, entries):
    center = totals[0:1] * (1.0 / entries)
    return center, lax.rsqrt(totals[1:2] * (1.0 / entries) - center * center + epsilon)


def layer_kernel(number, parts, batch_entries, kind, cut, *refs):
    state, weights, gains, offsets = refs[:4]
    totals = refs[4 : 4 + parts]
    refs = refs[4 + parts :]
    position = lax.axis_index("depth")
    if kind == "first":
        initial, initial_totals = refs[0], refs[1 : 1 + lax.axis_size("batch")]
        outs, taps = refs[1 + len(initial_totals) : -1], refs[-1]
    elif kind == "last":
        coarse_begin, terms = refs[:2]
        outs, taps = refs[2:-1], refs[-1]
    else:
        outs, taps = refs[:-1], refs[-1]
    samples, rows, width, channels = state.shape
    entries = rows * width

    def load(i):
        values = state[i]
        if kind == "first":
            values = jnp.where(position == 0, initial[i], values)
        return values.reshape(entries, channels)

    def added(pieces):
        summed = pieces[0][...]
        for piece in pieces[1:]:
            summed = summed + piece[...]
        return summed

    summed = added(totals)
    if kind == "first":
        summed = jnp.where(position == 0, added(initial_totals), summed)
    center, inverse = statistics(summed, batch_entries)
    scale = gains[number : number + 1] * inverse
    offset = offsets[number : number + 1]
    for i in range(samples):
        lay_out(jnp.maximum((load(i) - center) * scale + offset, 0.0), taps.at[i], width)
    total = jnp.zeros((2, channels), jnp.float32)
    for i in range(samples):
        change = convolved(taps.at[i], lambda row: weights[number, row], width, entries)
        values = load(i)
        made = values + fine_step * change
        if kind == "last":
            begun = coarse_begin[i].reshape(entries, channels)
            forcing = made - begun
            outs[0][i] = (begun + forcing).reshape(rows, width, channels)
            outs[1][i] = forcing
        else:
            outs[0][i] = made.reshape(rows, width, channels)
            total += both_sums(made)
            if kind == "first":
                outs[2][i] = (values + coarse_step * change).reshape(rows, width, channels)
    if kind == "last":
        half = samples // 2
        other = (1 - position % 2) * half
        for i in range(half):
            sent = jnp.where(
                position == 1, outs[0][other + i].reshape(entries, channels), outs[1][other + i]
            )
            for (low, high), out in zip(spans(cut, rows), outs[2:]):
                size = (high - low) * width
                out[i * size : (i + 1) * size] = sent[low * width : high * width]
        outs[2][half * cut[0] * width :] = terms[...]
    else:
        outs[1][...] = total
    if kind == "first":
        outs[3][...] = jnp.concatenate(
            [center, scale, offset, jnp.zeros((5, channels), jnp.float32)], axis=0
        )


def layer(number, state, weights, gains, offsets, totals, batch_entries, kind, extra=(), cut=None):
    samples, rows, width, channels = state.shape
    entries = rows * width
    half = samples // 2
    if kind == "last":
        outs = (
            f32(*state.shape),
            f32(samples, entries, channels),
            *(
                f32(half * (high - low) * width + (8 if low == 0 else 0), channels)
                for low, high in spans(cut, rows)
            ),
        )
    else:
        outs = (f32(*state.shape), f32(2, channels))
        if kind == "first":
            outs += (f32(*state.shape), f32(8, channels))
    return call(
        functools.partial(layer_kernel, number, len(totals), batch_entries, kind, cut),
        (state, weights, gains, offsets, *totals, *extra),
        outs,
        [pltpu.VMEM((samples, entries + 2 * width, 3 * channels), jnp.bfloat16)],
        flops=2 * samples * entries * 9 * channels * channels,
        moved=4 * samples * entries * channels,
    )


def widen_kernel(part, weights, after, out, held, done):
    piece = out.shape[0] // 3
    at = pl.multiple_of((lax.axis_index("batch") % 2) * 2 * piece + part * piece, piece)
    copy = pltpu.make_async_copy(weights.at[0, :, pl.ds(at, piece)], held, done)
    copy.start()
    copy.wait()
    for row in range(3):
        out[row * piece : (row + 1) * piece] = held[row].astype(jnp.float32)


def widen(part, weights, after):
    inner, channels = weights.shape[2:]
    piece = inner // 4
    return call(
        functools.partial(widen_kernel, part),
        (weights, after),
        f32(3 * piece, channels),
        [pltpu.VMEM((3, piece, channels), jnp.bfloat16), pltpu.SemaphoreType.DMA],
        specs=[in_place, whole],
        moved=3 * piece * channels * 6,
    )


def gather_kernel(weights, near_upper, near_lower, far_upper, far_lower, out):
    parity, core = lax.axis_index("depth") % 2, lax.axis_index("batch") % 2
    piece = near_upper.shape[0] // 3
    out[parity] = weights[0]
    for part, pieces in enumerate(((near_upper, far_upper), (near_lower, far_lower))):
        for owner, source in ((core, pieces[0]), (1 - core, pieces[1])):
            at = pl.multiple_of(owner * 2 * piece + part * piece, piece)
            for row in range(3):
                values = source[row * piece : (row + 1) * piece]
                out[1 - parity, row, pl.ds(at, piece)] = values.astype(jnp.bfloat16)


def relay_kernel(low, high, received, early, out):
    half, rows, width, channels = out.shape
    entries = rows * width
    odd = lax.axis_index("depth") % 2 == 1
    for i in range(half):
        passed = received[i * entries : (i + 1) * entries].reshape(rows, width, channels)
        out[i] = jnp.where(odd, early[half + i, low:high], passed)


def pair_kernel(turn, piece, cuts, start_cuts, kept, out_cuts, last, *refs):
    refs, taps = list(refs[:-1]), refs[-1]
    take = lambda count: [refs.pop(0) for _ in range(count)]
    pieces = len(cuts) + 1
    is_last = piece is None or piece == pieces - 1
    if piece is None:
        incoming, halo = take(pieces), []
    elif piece == 0:
        incoming, halo = take(1), []
    else:
        incoming, halo = take(2), take(1)
    exchange = take(pieces if piece is None else piece + 1)
    forcing, terms, kernels = take(3)
    take(1 + len(kept))
    gives = {low_high: ref for low_high, ref in zip(kept, refs[len(refs) - len(kept) :])}
    own = refs[len(refs) - len(kept) - 1]
    made = refs[: len(refs) - len(kept) - 1]
    half, height, width, channels = own.shape
    position = lax.axis_index("depth")
    parity = position % 2

    def flat(values):
        return values.reshape(-1, channels)

    def joined(values):
        return values[0] if len(values) == 1 else jnp.concatenate(values, axis=0)

    def forced(stage, i, low, high):
        here = forcing[parity * half + i, low * width : high * width]
        there = []
        for (first, end), ref in zip(spans(start_cuts, height), exchange):
            a, b = max(low, first), min(high, end)
            if a < b:
                base = i * (end - first) - first
                there.append(ref[(base + a) * width : (base + b) * width])
        return jnp.where(parity == stage, here, joined(there))

    def mapped(stage, i, values, begin, low, high):
        base = half * start_cuts[0] * width
        center, scale, offset = (
            jnp.where(parity == stage, terms[n : n + 1], exchange[0][base + n : base + n + 1])
            for n in range(3)
        )
        lay_out(
            jnp.maximum((values - center) * scale + offset, 0.0),
            taps.at[i, stage],
            width,
            low == 0,
            high == height,
        )
        change = convolved(
            taps.at[i, stage], lambda row: kernels[stage, row], width, (high - low) * width
        )
        kept_values = values[(low - begin) * width : (high - begin) * width]
        return kept_values + coarse_step * change + forced(stage, i, low, high)

    def put(i, low, values, is_own):
        high = low + values.shape[0] // width
        values = values.reshape(high - low, width, channels)
        if is_own:
            own[i, low:high] = values
            return
        for (first, end), ref in gives.items():
            a, b = max(low, first), min(high, end)
            if a < b:
                ref[i, a - first : b - first] = values[a - low : b - low]

    @pl.when(position // 2 == turn)
    def _():
        for i in range(half):
            if halo:
                cut = cuts[piece - 1]
                low = (cut - 1, cut - 2)
                values = joined([flat(incoming[0][i, -2:]), flat(incoming[1][i])])
                begin = (cut - 2, cut - 3)
            else:
                low, begin = (0, 0), (0, 0)
                values = joined([flat(part[i]) for part in incoming])
            high = (height, height) if is_last else (cuts[piece] - 1, cuts[piece] - 2)
            first = mapped(0, i, values, begin[0], low[0], high[0])
            values = joined([flat(halo[0][i, -2:]), first]) if halo else first
            second = mapped(1, i, values, begin[1], low[1], high[1])
            outs = list(made)
            if not is_last:
                outs.pop(0)[i] = first.reshape(-1, width, channels)
            if not last:
                for a, b in spans(out_cuts, height) if piece is None else [(low[1], high[1])]:
                    at = slice((a - low[1]) * width, (b - low[1]) * width)
                    outs.pop(0)[i] = second[at].reshape(-1, width, channels)

            @pl.when(parity == 0)
            def _():
                put(i, low[0], first, True)
                put(i, low[1], second, False)

            @pl.when(parity == 1)
            def _():
                put(i, low[0], first, False)
                put(i, low[1], second, True)


def pair(turn, piece, cuts, start_cuts, out_cuts, last, incoming, exchange, shared, own, gives):
    half, height, width, channels = own.shape
    pieces = len(cuts) + 1
    is_last = piece is None or piece == pieces - 1
    rows = lambda low, high: f32(half, high - low, width, channels)
    made = []
    if not is_last:
        low = cuts[piece - 1] - 1 if piece else 0
        made.append(rows(low, cuts[piece] - 1))
    if not last:
        if piece is None:
            made += [rows(*span) for span in spans(out_cuts, height)]
        else:
            made.append(rows(*spans(out_cuts, height)[piece]))
    kept = tuple(gives)
    carried = (own, *gives.values())
    operands = (*incoming, *exchange, *shared, *carried)
    count = len(operands) - len(carried)
    entries = half * height * width // pieces
    outs = call(
        functools.partial(pair_kernel, turn, piece, cuts, start_cuts, kept, out_cuts, last),
        operands,
        tuple(made) + tuple(f32(*part.shape) for part in carried),
        [pltpu.VMEM((half, 2, (height + 2) * width, 3 * channels), jnp.bfloat16)],
        aliases={count + n: len(made) + n for n in range(len(carried))},
        flops=4 * entries * 9 * channels * channels,
        moved=8 * entries * channels,
    )
    rest = outs[len(made) :]
    return outs[: len(made)], rest[0], dict(zip(kept, rest[1:]))


def finish_own_kernel(early, own, out, done):
    half = own.shape[0]
    position = lax.axis_index("depth")

    @pl.when(position < 2)
    def _():
        copy = pltpu.make_async_copy(early, out, done)
        copy.start()
        copy.wait()

    @pl.when(position >= 2)
    def _():
        copy = pltpu.make_async_copy(own, out.at[pl.ds((position % 2) * half, half)], done)
        copy.start()
        copy.wait()


def finish_kernel(cuts, *refs):
    pieces, out, done = refs[: len(cuts) + 1], refs[-2], refs[-1]
    half = pieces[0].shape[0]
    position = lax.axis_index("depth")

    @pl.when(position >= 2)
    def _():
        there = pl.ds((1 - position % 2) * half, half)
        copies = [
            pltpu.make_async_copy(piece, out.at[there, low:high], done.at[n])
            for n, (piece, (low, high)) in enumerate(zip(pieces, spans(cuts, out.shape[1])))
        ]
        for copy in copies:
            copy.start()
        for copy in copies:
            copy.wait()


def turns_of(count, height):
    start = (height // 2, height * 7 // 8)
    plan, cuts = [], start
    for _ in range(count):
        split = cuts[0] >= 3
        plan.append((cuts, split, tuple(cut - 2 for cut in cuts) if split else start))
        cuts = plan[-1][2]
    return start, plan


def steps(iterate, weights, norm_scale, norm_shift):
    initial = iterate[0]
    samples, rows, width, channels = initial.shape
    half = samples // 2
    devices = lax.axis_size("depth")
    group = lax.axis_size("batch")
    batch_entries = samples * rows * width * group
    weights = weights.reshape(layers_of_block, 3, 3 * channels, channels)
    run = functools.partial(layer, batch_entries=batch_entries)

    def gathered(sums, mark=False, ready=()):
        others = [
            lax.ppermute(sums, "batch", [(i, i ^ m) for i in range(group)])
            for m in range(1, group)
        ]
        if mark:
            sums = call(copy_kernel, (sums, *ready), f32(*sums.shape))
        return (sums, *others)

    partners = [(i, i ^ 1) for i in range(devices)]
    cores = [(i, i ^ 1) for i in range(group)]
    onward = [(i, i + 1) for i in range(devices - 1)]

    sums = call(sums_kernel, (initial,), f32(2, channels), moved=initial.size * 4)
    first_totals = gathered(sums, True, (weights, norm_scale, norm_shift))
    norms = (weights, norm_scale, norm_shift)
    current, totals = initial, first_totals
    for number in range(layers_of_block):
        current, sums = run(number, current, *norms, totals, kind="plain")
        if number == 0:
            near_upper = lax.ppermute(widen(0, weights, sums), "depth", partners)
        totals = gathered(sums, number == 0)
    arrived = lax.ppermute(current, "depth", onward)
    arrived_totals = lax.ppermute(sum(totals[1:], totals[0]), "depth", onward)

    start, plan = turns_of(devices // 2 - 1, rows)
    current, sums, coarse_begin, terms = run(
        0, arrived, *norms, (arrived_totals,), kind="first", extra=(initial, *first_totals)
    )
    near_lower = lax.ppermute(widen(1, weights, sums), "depth", partners)
    far_upper = lax.ppermute(near_upper, "batch", cores)
    for number in range(1, layers_of_block - 1):
        totals = gathered(sums, number == 1)
        current, sums = run(number, current, *norms, totals, kind="plain")
    far_lower = lax.ppermute(near_lower, "batch", cores)
    early, forcing, *sent = run(
        layers_of_block - 1,
        current,
        *norms,
        gathered(sums, True),
        kind="last",
        extra=(coarse_begin, terms),
        cut=start,
    )
    kernels = call(
        gather_kernel,
        (weights, near_upper, near_lower, far_upper, far_lower),
        jax.ShapeDtypeStruct((2, 3, 3 * channels, channels), jnp.bfloat16),
        moved=9 * channels * channels * 8,
    )

    exchange = [lax.ppermute(part, "depth", partners) for part in sent]
    passed = [
        call(
            functools.partial(relay_kernel, low, high),
            (part, early),
            f32(half, high - low, width, channels),
            moved=half * (high - low) * width * channels * 8,
        )
        for part, (low, high) in zip(exchange, spans(start, rows))
    ]
    own = jnp.zeros((half, rows, width, channels), jnp.float32)
    gives = {
        (low, high): jnp.zeros((half, high - low, width, channels), jnp.float32)
        for low, high in spans(plan[-1][2], rows)
    }
    back_spans = list(gives)
    back = []
    shared = (forcing, terms, kernels)
    for turn, (cuts, split, out_cuts) in enumerate(plan, 1):
        across = {2 * turn - 2: 2 * turn, 2 * turn - 1: 2 * turn + 1}
        across.update({b: a for a, b in across.items()})
        route = [(i, across.get(i, i ^ 1)) for i in range(devices)]
        arriving = [lax.ppermute(part, "depth", route) for part in passed]
        last = turn == len(plan)
        if not split:
            passed, own, gives = pair(
                turn, None, cuts, start, out_cuts, last, arriving, exchange, shared, own, gives
            )
            continue
        passed, halo = [], ()
        for n in range(len(cuts) + 1):
            incoming = (*arriving[max(n - 1, 0) : n + 1], *halo)
            now = {span: gives[span] for span in back_spans[n : n + 2]} if last else gives
            made, own, now = pair(
                turn,
                n,
                cuts,
                start,
                out_cuts,
                last,
                incoming,
                exchange[: n + 1],
                shared,
                own,
                now,
            )
            gives = {**gives, **now}
            halo = tuple(made[:1]) if n < len(cuts) else ()
            if last:
                back.append(lax.ppermute(gives[back_spans[n]], "depth", partners))
            else:
                passed.append(made[-1])
    if not back:
        back = [lax.ppermute(part, "depth", partners) for part in gives.values()]
    out = call(
        finish_own_kernel,
        (early, own),
        f32(*initial.shape),
        [pltpu.SemaphoreType.DMA],
        out_specs=in_place,
        moved=initial.size * 8,
    )
    out = call(
        functools.partial(finish_kernel, plan[-1][2]),
        (*back, out),
        f32(*initial.shape),
        [pltpu.SemaphoreType.DMA((len(back),))],
        specs=[whole] * len(back) + [in_place],
        out_specs=in_place,
        aliases={len(back): 0},
        moved=initial.size * 4,
    )
    return out[None]


def solution(mesh):
    return jax.shard_map(
        steps,
        mesh=mesh,
        in_specs=(
            P("depth", "batch", None, None, None),
            P("depth", None, None, None, None),
            P("depth", None),
            P("depth", None),
        ),
        out_specs=P("depth", "batch", None, None, None),
        check_vma=False,
    )
```

```python
import functools
import jax
import jax.numpy as jnp
from jax import lax
from jax.experimental import pallas as pl
from jax.experimental.pallas import tpu as pltpu
from jax.sharding import PartitionSpec as P

fine_step = 0.125
coarse_step = 0.5
epsilon = 1e-05
layers_of_block = 4
vmem_bytes = 16 << 20


whole = pl.BlockSpec(memory_space=pltpu.VMEM)
in_place = pl.BlockSpec(memory_space=pltpu.HBM)


def call(
    body, operands, outs, scratch=(), specs=None, out_specs=None, aliases=None,
    flops=0, moved=0, limit=vmem_bytes,
):
    return pl.pallas_call(
        body,
        out_shape=outs,
        in_specs=[whole] * len(operands) if specs is None else specs,
        out_specs=jax.tree.map(lambda _: whole, outs) if out_specs is None else out_specs,
        scratch_shapes=list(scratch),
        input_output_aliases=aliases or {},
        compiler_params=pltpu.CompilerParams(vmem_limit_bytes=limit),
        cost_estimate=pl.CostEstimate(flops=flops, bytes_accessed=moved, transcendentals=0),
    )(*operands)


def f32(*shape):
    return jax.ShapeDtypeStruct(shape, jnp.float32)


def lay_out(activated, taps, width, above=True, below=True):
    entries, channels = activated.shape
    column = lax.broadcasted_iota(jnp.int32, (entries, 1), 0) % width
    before = jnp.where(column == 0, 0.0, pltpu.roll(activated, 1, 0))
    after = jnp.where(column == width - 1, 0.0, pltpu.roll(activated, entries - 1, 0))
    edge = jnp.zeros((width, 3 * channels), jnp.bfloat16)
    start = width if above else 0
    if above:
        taps[0:width] = edge
    if below:
        taps[start + entries : start + entries + width] = edge
    for place, values in enumerate((before, activated, after)):
        taps[start : start + entries, place * channels : (place + 1) * channels] = values.astype(
            jnp.bfloat16
        )


def convolved(taps, kernel, width, entries):
    total = jnp.dot(taps[0:entries], kernel(0), preferred_element_type=jnp.float32)
    for row in (1, 2):
        total += jnp.dot(
            taps[row * width : row * width + entries],
            kernel(row),
            preferred_element_type=jnp.float32,
        )
    return total


def both_sums(values):
    return jnp.concatenate(
        [jnp.sum(values, axis=0, keepdims=True), jnp.sum(values * values, axis=0, keepdims=True)],
        axis=0,
    )


def spans(cuts, rows):
    edges = (0, *cuts, rows)
    return list(zip(edges, edges[1:]))


def sums_kernel(state, sums):
    samples, rows, width, channels = state.shape
    total = jnp.zeros((2, channels), jnp.float32)
    for i in range(samples):
        total += both_sums(state[i].reshape(rows * width, channels))
    sums[...] = total


def copy_kernel(*refs):
    refs[-1][...] = refs[0][...]


def statistics(totals, entries):
    center = totals[0:1] * (1.0 / entries)
    return center, lax.rsqrt(totals[1:2] * (1.0 / entries) - center * center + epsilon)


def layer_kernel(number, count, keep, parts, batch_entries, kind, cut, *refs):
    states, refs = refs[:count], refs[count:]
    weights, gains, offsets = refs[:3]
    totals = refs[3 : 3 + parts]
    refs = refs[3 + parts :]
    position = lax.axis_index("depth")
    if kind == "first":
        initial, initial_totals = refs[0], refs[1 : 1 + lax.axis_size("batch")]
        outs, taps = refs[1 + len(initial_totals) : -1], refs[-1]
    elif kind == "last":
        coarse_begin, terms = refs[:2]
        outs, taps = refs[2:-1], refs[-1]
    else:
        outs, taps = refs[:-1], refs[-1]
    samples, rows, width, channels = states[0].shape
    entries = rows * width

    def load(i):
        values = states[i // samples][i % samples]
        if kind == "first":
            values = jnp.where(position == 0, initial[i], values)
        return values.reshape(entries, channels)

    def added(pieces):
        summed = pieces[0][...]
        for piece in pieces[1:]:
            summed = summed + piece[...]
        return summed

    summed = added(totals)
    if kind == "first":
        summed = jnp.where(position == 0, added(initial_totals), summed)
    center, inverse = statistics(summed, batch_entries)
    scale = gains[number : number + 1] * inverse
    offset = offsets[number : number + 1]
    for i in range(count * samples):
        lay_out(jnp.maximum((load(i) - center) * scale + offset, 0.0), taps.at[i], width)
    total = jnp.zeros((2, channels), jnp.float32)
    for i in range(count * samples):
        change = convolved(taps.at[i], lambda row: weights[number, row], width, entries)
        values = load(i)
        made = values + fine_step * change
        if kind == "last":
            begun = coarse_begin[i].reshape(entries, channels)
            forcing = made - begun
            outs[0][i] = (begun + forcing).reshape(rows, width, channels)
            outs[1][i] = forcing
        else:
            if i < keep * samples:
                outs[i // samples][i % samples] = made.reshape(rows, width, channels)
            total += both_sums(made)
            if kind == "first":
                outs[2][i] = (values + coarse_step * change).reshape(rows, width, channels)
    if kind == "last":
        half = samples // 2
        other = (1 - position % 2) * half
        for i in range(half):
            sent = jnp.where(
                position == 1, outs[0][other + i].reshape(entries, channels), outs[1][other + i]
            )
            for (low, high), out in zip(spans(cut, rows), outs[2:]):
                size = (high - low) * width
                out[i * size : (i + 1) * size] = sent[low * width : high * width]
        outs[2][half * cut[0] * width :] = terms[...]
    else:
        outs[keep][...] = total
    if kind == "first":
        outs[3][...] = jnp.concatenate(
            [center, scale, offset, jnp.zeros((5, channels), jnp.float32)], axis=0
        )


def layer(number, states, weights, gains, offsets, totals, batch_entries, kind, extra=(), cut=None, keep=None):
    state, keep = states[0], keep or len(states)
    samples, rows, width, channels = state.shape
    entries = rows * width
    half = samples // 2
    if kind == "last":
        outs = (
            f32(*state.shape),
            f32(samples, entries, channels),
            *(
                f32(half * (high - low) * width + (8 if low == 0 else 0), channels)
                for low, high in spans(cut, rows)
            ),
        )
    else:
        outs = (*(f32(*state.shape) for state in states[:keep]), f32(2, channels))
        if kind == "first":
            outs += (f32(*state.shape), f32(8, channels))
    return call(
        functools.partial(
            layer_kernel, number, len(states), keep, len(totals), batch_entries, kind, cut
        ),
        (*states, weights, gains, offsets, *totals, *extra),
        outs,
        [pltpu.VMEM((len(states) * samples, entries + 2 * width, 3 * channels), jnp.bfloat16)],
        flops=2 * len(states) * samples * entries * 9 * channels * channels,
        moved=4 * len(states) * samples * entries * channels,
    )


def widen_kernel(part, weights, after, out):
    piece = out.shape[0] // 3
    at = pl.multiple_of((lax.axis_index("batch") % 2) * 2 * piece + part * piece, piece)
    for row in range(3):
        out[row * piece : (row + 1) * piece] = weights[0, row, pl.ds(at, piece)].astype(jnp.float32)


def widen(part, weights, after):
    inner, channels = weights.shape[2:]
    piece = inner // 4
    return call(
        functools.partial(widen_kernel, part),
        (weights, after),
        f32(3 * piece, channels),
        moved=3 * piece * channels * 6,
    )


def stage_kernel(weights, out, done):
    copies = [
        pltpu.make_async_copy(weights.at[n], out.at[n], done.at[n]) for n in range(out.shape[0])
    ]
    for copy in copies:
        copy.start()
    for copy in copies:
        copy.wait()


def gather_kernel(weights, near_upper, near_lower, far_upper, far_lower, out):
    parity, core = lax.axis_index("depth") % 2, lax.axis_index("batch") % 2
    piece = near_upper.shape[0] // 3
    out[parity] = weights[0]
    for part, pieces in enumerate(((near_upper, far_upper), (near_lower, far_lower))):
        for owner, source in ((core, pieces[0]), (1 - core, pieces[1])):
            at = pl.multiple_of(owner * 2 * piece + part * piece, piece)
            for row in range(3):
                values = source[row * piece : (row + 1) * piece]
                out[1 - parity, row, pl.ds(at, piece)] = values.astype(jnp.bfloat16)


def relay_kernel(low, high, received, early, out):
    half, rows, width, channels = out.shape
    entries = rows * width
    odd = lax.axis_index("depth") % 2 == 1
    for i in range(half):
        passed = received[i * entries : (i + 1) * entries].reshape(rows, width, channels)
        out[i] = jnp.where(odd, early[half + i, low:high], passed)


def pair_kernel(turn, piece, cuts, start_cuts, kept, out_cuts, last, *refs):
    refs, taps = list(refs[:-1]), refs[-1]
    take = lambda count: [refs.pop(0) for _ in range(count)]
    pieces = len(cuts) + 1
    is_last = piece is None or piece == pieces - 1
    if piece is None:
        incoming, halo = take(pieces), []
    elif piece == 0:
        incoming, halo = take(1), []
    else:
        incoming, halo = take(2), take(1)
    exchange = take(pieces if piece is None else piece + 1)
    forcing, terms, kernels = take(3)
    take(1 + len(kept))
    gives = {low_high: ref for low_high, ref in zip(kept, refs[len(refs) - len(kept) :])}
    own = refs[len(refs) - len(kept) - 1]
    made = refs[: len(refs) - len(kept) - 1]
    half, height, width, channels = own.shape
    position = lax.axis_index("depth")
    parity = position % 2

    def flat(values):
        return values.reshape(-1, channels)

    def joined(values):
        return values[0] if len(values) == 1 else jnp.concatenate(values, axis=0)

    def forced(stage, i, low, high):
        here = forcing[parity * half + i, low * width : high * width]
        there = []
        for (first, end), ref in zip(spans(start_cuts, height), exchange):
            a, b = max(low, first), min(high, end)
            if a < b:
                base = i * (end - first) - first
                there.append(ref[(base + a) * width : (base + b) * width])
        return jnp.where(parity == stage, here, joined(there))

    def mapped(stage, i, values, begin, low, high):
        base = half * start_cuts[0] * width
        center, scale, offset = (
            jnp.where(parity == stage, terms[n : n + 1], exchange[0][base + n : base + n + 1])
            for n in range(3)
        )
        lay_out(
            jnp.maximum((values - center) * scale + offset, 0.0),
            taps.at[i, stage],
            width,
            low == 0,
            high == height,
        )
        change = convolved(
            taps.at[i, stage], lambda row: kernels[stage, row], width, (high - low) * width
        )
        kept_values = values[(low - begin) * width : (high - begin) * width]
        return kept_values + coarse_step * change + forced(stage, i, low, high)

    def put(i, low, values, is_own):
        high = low + values.shape[0] // width
        values = values.reshape(high - low, width, channels)
        if is_own:
            own[i, low:high] = values
            return
        for (first, end), ref in gives.items():
            a, b = max(low, first), min(high, end)
            if a < b:
                ref[i, a - first : b - first] = values[a - low : b - low]

    @pl.when(position // 2 == turn)
    def _():
        for i in range(half):
            if halo:
                cut = cuts[piece - 1]
                low = (cut - 1, cut - 2)
                values = joined([flat(incoming[0][i, -2:]), flat(incoming[1][i])])
                begin = (cut - 2, cut - 3)
            else:
                low, begin = (0, 0), (0, 0)
                values = joined([flat(part[i]) for part in incoming])
            high = (height, height) if is_last else (cuts[piece] - 1, cuts[piece] - 2)
            first = mapped(0, i, values, begin[0], low[0], high[0])
            values = joined([flat(halo[0][i, -2:]), first]) if halo else first
            second = mapped(1, i, values, begin[1], low[1], high[1])
            outs = list(made)
            if not is_last:
                outs.pop(0)[i] = first.reshape(-1, width, channels)
            if not last:
                for a, b in spans(out_cuts, height) if piece is None else [(low[1], high[1])]:
                    at = slice((a - low[1]) * width, (b - low[1]) * width)
                    outs.pop(0)[i] = second[at].reshape(-1, width, channels)

            @pl.when(parity == 0)
            def _():
                put(i, low[0], first, True)
                put(i, low[1], second, False)

            @pl.when(parity == 1)
            def _():
                put(i, low[0], first, False)
                put(i, low[1], second, True)


def pair(turn, piece, cuts, start_cuts, out_cuts, last, incoming, exchange, shared, own, gives):
    half, height, width, channels = own.shape
    pieces = len(cuts) + 1
    is_last = piece is None or piece == pieces - 1
    rows = lambda low, high: f32(half, high - low, width, channels)
    made = []
    if not is_last:
        low = cuts[piece - 1] - 1 if piece else 0
        made.append(rows(low, cuts[piece] - 1))
    if not last:
        if piece is None:
            made += [rows(*span) for span in spans(out_cuts, height)]
        else:
            made.append(rows(*spans(out_cuts, height)[piece]))
    kept = tuple(gives)
    carried = (own, *gives.values())
    operands = (*incoming, *exchange, *shared, *carried)
    count = len(operands) - len(carried)
    entries = half * height * width // pieces
    outs = call(
        functools.partial(pair_kernel, turn, piece, cuts, start_cuts, kept, out_cuts, last),
        operands,
        tuple(made) + tuple(f32(*part.shape) for part in carried),
        [pltpu.VMEM((half, 2, (height + 2) * width, 3 * channels), jnp.bfloat16)],
        aliases={count + n: len(made) + n for n in range(len(carried))},
        flops=4 * entries * 9 * channels * channels,
        moved=8 * entries * channels,
    )
    rest = outs[len(made) :]
    return outs[: len(made)], rest[0], dict(zip(kept, rest[1:]))


def finish_own_kernel(early, own, out, done):
    half = own.shape[0]
    position = lax.axis_index("depth")

    @pl.when(position < 2)
    def _():
        copy = pltpu.make_async_copy(early, out, done)
        copy.start()
        copy.wait()

    @pl.when(position >= 2)
    def _():
        copy = pltpu.make_async_copy(own, out.at[pl.ds((position % 2) * half, half)], done)
        copy.start()
        copy.wait()


def finish_kernel(cuts, *refs):
    pieces, out, done = refs[: len(cuts) + 1], refs[-2], refs[-1]
    half = pieces[0].shape[0]
    position = lax.axis_index("depth")

    @pl.when(position >= 2)
    def _():
        there = pl.ds((1 - position % 2) * half, half)
        copies = [
            pltpu.make_async_copy(piece, out.at[there, low:high], done.at[n])
            for n, (piece, (low, high)) in enumerate(zip(pieces, spans(cuts, out.shape[1])))
        ]
        for copy in copies:
            copy.start()
        for copy in copies:
            copy.wait()


def turns_of(count, height):
    start = (height // 2, height * 7 // 8)
    plan, cuts = [], start
    for _ in range(count):
        split = cuts[0] >= 3
        plan.append((cuts, split, tuple(cut - 2 for cut in cuts) if split else start))
        cuts = plan[-1][2]
    return start, plan


def steps(iterate, weights, norm_scale, norm_shift):
    initial = iterate[0]
    samples, rows, width, channels = initial.shape
    half = samples // 2
    devices = lax.axis_size("depth")
    group = lax.axis_size("batch")
    batch_entries = samples * rows * width * group
    weights = weights.reshape(layers_of_block, 3, 3 * channels, channels)
    run = functools.partial(layer, batch_entries=batch_entries)

    def gathered(sums, mark=False, chips=False, ready=()):
        others = [
            lax.ppermute(sums, "batch", [(i, i ^ m) for i in range(group)])
            for m in (range(2, group, 2) if chips else range(1, group))
        ]
        if mark:
            sums = call(copy_kernel, (sums, *ready), f32(*sums.shape))
        return (sums, *others)

    partners = [(i, i ^ 1) for i in range(devices)]
    cores = [(i, i ^ 1) for i in range(group)]
    onward = [(i, i + 1) for i in range(devices - 1)]

    sums = call(sums_kernel, (initial,), f32(2, channels), moved=initial.size * 4)
    first_totals = gathered(sums)
    other = lax.ppermute(initial, "batch", cores)
    weights = call(
        stage_kernel,
        (weights,),
        jax.ShapeDtypeStruct(weights.shape, weights.dtype),
        [pltpu.SemaphoreType.DMA((layers_of_block,))],
        specs=[in_place],
        moved=weights.size * 4,
        limit=47 << 20,
    )
    norms = (weights, norm_scale, norm_shift)
    states, totals = (initial, other), first_totals
    for number in range(layers_of_block - 1):
        keep = 2 if number < layers_of_block - 2 else 1
        *states, sums = run(number, states, *norms, totals, kind="plain", keep=keep)
        if number == 0:
            near_upper = lax.ppermute(widen(0, weights, sums), "depth", partners)
        totals = gathered(sums, number == 0, True)
    current, sums = run(layers_of_block - 1, states[:1], *norms, totals, kind="plain")
    totals = gathered(sums)
    arrived = lax.ppermute(current, "depth", onward)
    arrived_totals = lax.ppermute(sum(totals[1:], totals[0]), "depth", onward)

    start, plan = turns_of(devices // 2 - 1, rows)
    current, sums, coarse_begin, terms = run(
        0, (arrived,), *norms, (arrived_totals,), kind="first", extra=(initial, *first_totals)
    )
    other = lax.ppermute(current, "batch", cores)
    near_lower = lax.ppermute(widen(1, weights, sums), "depth", partners)
    far_upper = lax.ppermute(near_upper, "batch", cores)
    states = (current, other)
    for number in range(1, layers_of_block - 1):
        totals = gathered(sums, number == 2, number > 1)
        keep = 2 if number < layers_of_block - 2 else 1
        *states, sums = run(number, states, *norms, totals, kind="plain", keep=keep)
    far_lower = lax.ppermute(near_lower, "batch", cores)
    early, forcing, *sent = run(
        layers_of_block - 1,
        states[:1],
        *norms,
        gathered(sums, True, True),
        kind="last",
        extra=(coarse_begin, terms),
        cut=start,
    )
    kernels = call(
        gather_kernel,
        (weights, near_upper, near_lower, far_upper, far_lower),
        jax.ShapeDtypeStruct((2, 3, 3 * channels, channels), jnp.bfloat16),
        moved=9 * channels * channels * 8,
    )

    exchange = [lax.ppermute(part, "depth", partners) for part in sent]
    passed = [
        call(
            functools.partial(relay_kernel, low, high),
            (part, early),
            f32(half, high - low, width, channels),
            moved=half * (high - low) * width * channels * 8,
        )
        for part, (low, high) in zip(exchange, spans(start, rows))
    ]
    own = jnp.zeros((half, rows, width, channels), jnp.float32)
    gives = {
        (low, high): jnp.zeros((half, high - low, width, channels), jnp.float32)
        for low, high in spans(plan[-1][2], rows)
    }
    back_spans = list(gives)
    back = []
    shared = (forcing, terms, kernels)
    for turn, (cuts, split, out_cuts) in enumerate(plan, 1):
        across = {2 * turn - 2: 2 * turn, 2 * turn - 1: 2 * turn + 1}
        across.update({b: a for a, b in across.items()})
        route = [(i, across.get(i, i ^ 1)) for i in range(devices)]
        arriving = [lax.ppermute(part, "depth", route) for part in passed]
        last = turn == len(plan)
        if not split:
            passed, own, gives = pair(
                turn, None, cuts, start, out_cuts, last, arriving, exchange, shared, own, gives
            )
            continue
        passed, halo = [], ()
        for n in range(len(cuts) + 1):
            incoming = (*arriving[max(n - 1, 0) : n + 1], *halo)
            now = {span: gives[span] for span in back_spans[n : n + 2]} if last else gives
            made, own, now = pair(
                turn,
                n,
                cuts,
                start,
                out_cuts,
                last,
                incoming,
                exchange[: n + 1],
                shared,
                own,
                now,
            )
            gives = {**gives, **now}
            halo = tuple(made[:1]) if n < len(cuts) else ()
            if last:
                back.append(lax.ppermute(gives[back_spans[n]], "depth", partners))
            else:
                passed.append(made[-1])
    if not back:
        back = [lax.ppermute(part, "depth", partners) for part in gives.values()]
    out = call(
        finish_own_kernel,
        (early, own),
        f32(*initial.shape),
        [pltpu.SemaphoreType.DMA],
        out_specs=in_place,
        moved=initial.size * 8,
    )
    out = call(
        functools.partial(finish_kernel, plan[-1][2]),
        (*back, out),
        f32(*initial.shape),
        [pltpu.SemaphoreType.DMA((len(back),))],
        specs=[whole] * len(back) + [in_place],
        out_specs=in_place,
        aliases={len(back): 0},
        moved=initial.size * 4,
    )
    return out[None]


def solution(mesh):
    return jax.shard_map(
        steps,
        mesh=mesh,
        in_specs=(
            P("depth", "batch", None, None, None),
            P("depth", None, None, None, None),
            P("depth", None),
            P("depth", None),
        ),
        out_specs=P("depth", "batch", None, None, None),
        check_vma=False,
    )
```

```python
import functools
import jax
import jax.numpy as jnp
from jax import lax
from jax.experimental import pallas as pl
from jax.experimental.pallas import tpu as pltpu
from jax.sharding import PartitionSpec as P

fine_step = 0.125
coarse_step = 0.5
epsilon = 1e-05
layers_of_block = 4
vmem_bytes = 16 << 20


whole = pl.BlockSpec(memory_space=pltpu.VMEM)
in_place = pl.BlockSpec(memory_space=pltpu.HBM)


def call(
    body, operands, outs, scratch=(), specs=None, out_specs=None, aliases=None,
    flops=0, moved=0, limit=vmem_bytes,
):
    return pl.pallas_call(
        body,
        out_shape=outs,
        in_specs=[whole] * len(operands) if specs is None else specs,
        out_specs=jax.tree.map(lambda _: whole, outs) if out_specs is None else out_specs,
        scratch_shapes=list(scratch),
        input_output_aliases=aliases or {},
        compiler_params=pltpu.CompilerParams(vmem_limit_bytes=limit),
        cost_estimate=pl.CostEstimate(flops=flops, bytes_accessed=moved, transcendentals=0),
    )(*operands)


def f32(*shape):
    return jax.ShapeDtypeStruct(shape, jnp.float32)


def lay_out(activated, taps, width, above=True, below=True):
    entries, channels = activated.shape
    column = lax.broadcasted_iota(jnp.int32, (entries, 1), 0) % width
    before = jnp.where(column == 0, 0.0, pltpu.roll(activated, 1, 0))
    after = jnp.where(column == width - 1, 0.0, pltpu.roll(activated, entries - 1, 0))
    edge = jnp.zeros((width, 3 * channels), jnp.bfloat16)
    start = width if above else 0
    if above:
        taps[0:width] = edge
    if below:
        taps[start + entries : start + entries + width] = edge
    for place, values in enumerate((before, activated, after)):
        taps[start : start + entries, place * channels : (place + 1) * channels] = values.astype(
            jnp.bfloat16
        )


def convolved(taps, kernel, width, entries):
    total = jnp.dot(taps[0:entries], kernel(0), preferred_element_type=jnp.float32)
    for row in (1, 2):
        total += jnp.dot(
            taps[row * width : row * width + entries],
            kernel(row),
            preferred_element_type=jnp.float32,
        )
    return total


def both_sums(values):
    return jnp.concatenate(
        [jnp.sum(values, axis=0, keepdims=True), jnp.sum(values * values, axis=0, keepdims=True)],
        axis=0,
    )


def spans(cuts, rows):
    edges = (0, *cuts, rows)
    return list(zip(edges, edges[1:]))


def sums_kernel(state, held, sums):
    samples, rows, width, channels = state.shape
    total = jnp.zeros((2, channels), jnp.float32)
    for i in range(samples):
        held[i] = state[i]
        total += both_sums(state[i].reshape(rows * width, channels))
    sums[...] = total


def copy_kernel(*refs):
    refs[-1][...] = refs[0][...]


def statistics(totals, entries):
    center = totals[0:1] * (1.0 / entries)
    return center, lax.rsqrt(totals[1:2] * (1.0 / entries) - center * center + epsilon)


def layer_kernel(number, count, keep, parts, batch_entries, kind, cut, *refs):
    states, refs = refs[:count], refs[count:]
    weights, gains, offsets = refs[:3]
    totals = refs[3 : 3 + parts]
    refs = refs[3 + parts :]
    position = lax.axis_index("depth")
    if kind == "first":
        initial, initial_totals = refs[0], refs[1 : 1 + lax.axis_size("batch")]
        outs, taps = refs[1 + len(initial_totals) : -1], refs[-1]
    elif kind == "last":
        coarse_begin, terms = refs[:2]
        outs, taps = refs[2:-1], refs[-1]
    else:
        outs, taps = refs[:-1], refs[-1]
    samples, rows, width, channels = states[0].shape
    entries = rows * width

    def load(i):
        values = states[i // samples][i % samples]
        if kind == "first":
            values = jnp.where(position == 0, initial[i], values)
        return values.reshape(entries, channels)

    def added(pieces):
        summed = pieces[0][...]
        for piece in pieces[1:]:
            summed = summed + piece[...]
        return summed

    summed = added(totals)
    if kind == "first":
        summed = jnp.where(position == 0, added(initial_totals), summed)
    center, inverse = statistics(summed, batch_entries)
    scale = gains[number : number + 1] * inverse
    offset = offsets[number : number + 1]
    for i in range(count * samples):
        lay_out(jnp.maximum((load(i) - center) * scale + offset, 0.0), taps.at[i], width)
    total = jnp.zeros((2, channels), jnp.float32)
    for i in range(count * samples):
        change = convolved(taps.at[i], lambda row: weights[number, row], width, entries)
        values = load(i)
        made = values + fine_step * change
        if kind == "last":
            begun = coarse_begin[i].reshape(entries, channels)
            forcing = made - begun
            outs[0][i] = (begun + forcing).reshape(rows, width, channels)
            outs[1][i] = forcing
        else:
            if i < keep * samples:
                outs[i // samples][i % samples] = made.reshape(rows, width, channels)
            total += both_sums(made)
            if kind == "first":
                outs[2][i] = (values + coarse_step * change).reshape(rows, width, channels)
    if kind == "last":
        half = samples // 2
        other = (1 - position % 2) * half
        for i in range(half):
            sent = jnp.where(
                position == 1, outs[0][other + i].reshape(entries, channels), outs[1][other + i]
            )
            for (low, high), out in zip(spans(cut, rows), outs[2:]):
                size = (high - low) * width
                out[i * size : (i + 1) * size] = sent[low * width : high * width]
        outs[2][half * cut[0] * width :] = terms[...]
    else:
        outs[keep][...] = total
    if kind == "first":
        outs[3][...] = jnp.concatenate(
            [center, scale, offset, jnp.zeros((5, channels), jnp.float32)], axis=0
        )


def layer(number, states, weights, gains, offsets, totals, batch_entries, kind, extra=(), cut=None, keep=None):
    state, keep = states[0], keep or len(states)
    samples, rows, width, channels = state.shape
    entries = rows * width
    half = samples // 2
    if kind == "last":
        outs = (
            f32(*state.shape),
            f32(samples, entries, channels),
            *(
                f32(half * (high - low) * width + (8 if low == 0 else 0), channels)
                for low, high in spans(cut, rows)
            ),
        )
    else:
        outs = (*(f32(*state.shape) for state in states[:keep]), f32(2, channels))
        if kind == "first":
            outs += (f32(*state.shape), f32(8, channels))
    return call(
        functools.partial(
            layer_kernel, number, len(states), keep, len(totals), batch_entries, kind, cut
        ),
        (*states, weights, gains, offsets, *totals, *extra),
        outs,
        [pltpu.VMEM((len(states) * samples, entries + 2 * width, 3 * channels), jnp.bfloat16)],
        flops=2 * len(states) * samples * entries * 9 * channels * channels,
        moved=4 * len(states) * samples * entries * channels,
    )


def widen_kernel(part, weights, after, out):
    piece = out.shape[0] // 3
    at = pl.multiple_of((lax.axis_index("batch") % 2) * 2 * piece + part * piece, piece)
    for row in range(3):
        out[row * piece : (row + 1) * piece] = weights[0, row, pl.ds(at, piece)].astype(jnp.float32)


def widen(part, weights, after):
    inner, channels = weights.shape[2:]
    piece = inner // 4
    return call(
        functools.partial(widen_kernel, part),
        (weights, after),
        f32(3 * piece, channels),
        moved=3 * piece * channels * 6,
    )


def stage_kernel(weights, out, done):
    copies = [
        pltpu.make_async_copy(weights.at[n], out.at[n], done.at[n]) for n in range(out.shape[0])
    ]
    for copy in copies:
        copy.start()
    for copy in copies:
        copy.wait()


def gather_kernel(weights, near_upper, near_lower, far_upper, far_lower, out):
    parity, core = lax.axis_index("depth") % 2, lax.axis_index("batch") % 2
    piece = near_upper.shape[0] // 3
    out[parity] = weights[0]
    for part, pieces in enumerate(((near_upper, far_upper), (near_lower, far_lower))):
        for owner, source in ((core, pieces[0]), (1 - core, pieces[1])):
            at = pl.multiple_of(owner * 2 * piece + part * piece, piece)
            for row in range(3):
                values = source[row * piece : (row + 1) * piece]
                out[1 - parity, row, pl.ds(at, piece)] = values.astype(jnp.bfloat16)


def relay_kernel(low, high, received, early, out):
    half, rows, width, channels = out.shape
    entries = rows * width
    odd = lax.axis_index("depth") % 2 == 1
    for i in range(half):
        passed = received[i * entries : (i + 1) * entries].reshape(rows, width, channels)
        out[i] = jnp.where(odd, early[half + i, low:high], passed)


def pair_kernel(turn, piece, cuts, start_cuts, kept, out_cuts, last, *refs):
    refs, taps = list(refs[:-1]), refs[-1]
    take = lambda count: [refs.pop(0) for _ in range(count)]
    pieces = len(cuts) + 1
    is_last = piece is None or piece == pieces - 1
    if piece is None:
        incoming, halo = take(pieces), []
    elif piece == 0:
        incoming, halo = take(1), []
    else:
        incoming, halo = take(2), take(1)
    exchange = take(pieces if piece is None else piece + 1)
    forcing, terms, kernels = take(3)
    take(1 + len(kept))
    gives = {low_high: ref for low_high, ref in zip(kept, refs[len(refs) - len(kept) :])}
    own = refs[len(refs) - len(kept) - 1]
    made = refs[: len(refs) - len(kept) - 1]
    half, height, width, channels = own.shape
    position = lax.axis_index("depth")
    parity = position % 2

    def flat(values):
        return values.reshape(-1, channels)

    def joined(values):
        return values[0] if len(values) == 1 else jnp.concatenate(values, axis=0)

    def forced(stage, i, low, high):
        here = forcing[parity * half + i, low * width : high * width]
        there = []
        for (first, end), ref in zip(spans(start_cuts, height), exchange):
            a, b = max(low, first), min(high, end)
            if a < b:
                base = i * (end - first) - first
                there.append(ref[(base + a) * width : (base + b) * width])
        return jnp.where(parity == stage, here, joined(there))

    def mapped(stage, i, values, begin, low, high):
        base = half * start_cuts[0] * width
        center, scale, offset = (
            jnp.where(parity == stage, terms[n : n + 1], exchange[0][base + n : base + n + 1])
            for n in range(3)
        )
        lay_out(
            jnp.maximum((values - center) * scale + offset, 0.0),
            taps.at[i, stage],
            width,
            low == 0,
            high == height,
        )
        change = convolved(
            taps.at[i, stage], lambda row: kernels[stage, row], width, (high - low) * width
        )
        kept_values = values[(low - begin) * width : (high - begin) * width]
        return kept_values + coarse_step * change + forced(stage, i, low, high)

    def put(i, low, values, is_own):
        high = low + values.shape[0] // width
        values = values.reshape(high - low, width, channels)
        if is_own:
            own[i, low:high] = values
            return
        for (first, end), ref in gives.items():
            a, b = max(low, first), min(high, end)
            if a < b:
                ref[i, a - first : b - first] = values[a - low : b - low]

    @pl.when(position // 2 == turn)
    def _():
        for i in range(half):
            if halo:
                cut = cuts[piece - 1]
                low = (cut - 1, cut - 2)
                values = joined([flat(incoming[0][i, -2:]), flat(incoming[1][i])])
                begin = (cut - 2, cut - 3)
            else:
                low, begin = (0, 0), (0, 0)
                values = joined([flat(part[i]) for part in incoming])
            high = (height, height) if is_last else (cuts[piece] - 1, cuts[piece] - 2)
            first = mapped(0, i, values, begin[0], low[0], high[0])
            values = joined([flat(halo[0][i, -2:]), first]) if halo else first
            second = mapped(1, i, values, begin[1], low[1], high[1])
            outs = list(made)
            if not is_last:
                outs.pop(0)[i] = first.reshape(-1, width, channels)
            if not last:
                for a, b in spans(out_cuts, height) if piece is None else [(low[1], high[1])]:
                    at = slice((a - low[1]) * width, (b - low[1]) * width)
                    outs.pop(0)[i] = second[at].reshape(-1, width, channels)

            @pl.when(parity == 0)
            def _():
                put(i, low[0], first, True)
                put(i, low[1], second, False)

            @pl.when(parity == 1)
            def _():
                put(i, low[0], first, False)
                put(i, low[1], second, True)


def pair(turn, piece, cuts, start_cuts, out_cuts, last, incoming, exchange, shared, own, gives):
    half, height, width, channels = own.shape
    pieces = len(cuts) + 1
    is_last = piece is None or piece == pieces - 1
    rows = lambda low, high: f32(half, high - low, width, channels)
    made = []
    if not is_last:
        low = cuts[piece - 1] - 1 if piece else 0
        made.append(rows(low, cuts[piece] - 1))
    if not last:
        if piece is None:
            made += [rows(*span) for span in spans(out_cuts, height)]
        else:
            made.append(rows(*spans(out_cuts, height)[piece]))
    kept = tuple(gives)
    carried = (own, *gives.values())
    operands = (*incoming, *exchange, *shared, *carried)
    count = len(operands) - len(carried)
    entries = half * height * width // pieces
    outs = call(
        functools.partial(pair_kernel, turn, piece, cuts, start_cuts, kept, out_cuts, last),
        operands,
        tuple(made) + tuple(f32(*part.shape) for part in carried),
        [pltpu.VMEM((half, 2, (height + 2) * width, 3 * channels), jnp.bfloat16)],
        aliases={count + n: len(made) + n for n in range(len(carried))},
        flops=4 * entries * 9 * channels * channels,
        moved=8 * entries * channels,
    )
    rest = outs[len(made) :]
    return outs[: len(made)], rest[0], dict(zip(kept, rest[1:]))


def finish_own_kernel(early, own, out, done):
    half = own.shape[0]
    position = lax.axis_index("depth")

    @pl.when(position < 2)
    def _():
        copy = pltpu.make_async_copy(early, out, done)
        copy.start()
        copy.wait()

    @pl.when(position >= 2)
    def _():
        copy = pltpu.make_async_copy(own, out.at[pl.ds((position % 2) * half, half)], done)
        copy.start()
        copy.wait()


def finish_kernel(cuts, *refs):
    pieces, out, done = refs[: len(cuts) + 1], refs[-2], refs[-1]
    half = pieces[0].shape[0]
    position = lax.axis_index("depth")

    @pl.when(position >= 2)
    def _():
        there = pl.ds((1 - position % 2) * half, half)
        copies = [
            pltpu.make_async_copy(piece, out.at[there, low:high], done.at[n])
            for n, (piece, (low, high)) in enumerate(zip(pieces, spans(cuts, out.shape[1])))
        ]
        for copy in copies:
            copy.start()
        for copy in copies:
            copy.wait()


def turns_of(count, height):
    start = (height // 2, height * 7 // 8)
    plan, cuts = [], start
    for _ in range(count):
        split = cuts[0] >= 3
        plan.append((cuts, split, tuple(cut - 2 for cut in cuts) if split else start))
        cuts = plan[-1][2]
    return start, plan


def steps(iterate, weights, norm_scale, norm_shift):
    initial = iterate[0]
    samples, rows, width, channels = initial.shape
    half = samples // 2
    devices = lax.axis_size("depth")
    group = lax.axis_size("batch")
    batch_entries = samples * rows * width * group
    weights = weights.reshape(layers_of_block, 3, 3 * channels, channels)
    run = functools.partial(layer, batch_entries=batch_entries)

    def gathered(sums, mark=False, chips=False, ready=()):
        others = [
            lax.ppermute(sums, "batch", [(i, i ^ m) for i in range(group)])
            for m in (range(3, group, 2) if chips else range(1, group))
        ]
        if mark:
            sums = call(copy_kernel, (sums, *ready), f32(*sums.shape))
        return (sums, *others)

    partners = [(i, i ^ 1) for i in range(devices)]
    cores = [(i, i ^ 1) for i in range(group)]
    onward = [(i, i + 1) for i in range(devices - 1)]

    initial, sums = call(
        sums_kernel, (initial,), (f32(*initial.shape), f32(2, channels)), moved=initial.size * 4
    )
    first_totals = gathered(sums)
    other = lax.ppermute(initial, "batch", cores)
    weights = call(
        stage_kernel,
        (weights,),
        jax.ShapeDtypeStruct(weights.shape, weights.dtype),
        [pltpu.SemaphoreType.DMA((layers_of_block,))],
        specs=[in_place],
        moved=weights.size * 4,
        limit=47 << 20,
    )
    norms = (weights, norm_scale, norm_shift)
    states, totals = (initial, other), first_totals
    for number in range(layers_of_block - 1):
        keep = 2 if number < layers_of_block - 2 else 1
        *states, sums = run(number, states, *norms, totals, kind="plain", keep=keep)
        if number == 0:
            near_upper = lax.ppermute(widen(0, weights, sums), "depth", partners)
        totals = gathered(sums, number == 0, True)
    current, sums = run(layers_of_block - 1, states[:1], *norms, totals, kind="plain")
    totals = gathered(sums)
    arrived = lax.ppermute(current, "depth", onward)
    arrived_totals = lax.ppermute(sum(totals[1:], totals[0]), "depth", onward)

    start, plan = turns_of(devices // 2 - 1, rows)
    current, sums, coarse_begin, terms = run(
        0, (arrived,), *norms, (arrived_totals,), kind="first", extra=(initial, *first_totals)
    )
    other = lax.ppermute(current, "batch", cores)
    near_lower = lax.ppermute(widen(1, weights, sums), "depth", partners)
    far_upper = lax.ppermute(near_upper, "batch", cores)
    states = (current, other)
    for number in range(1, layers_of_block - 1):
        totals = gathered(sums, number == 1, number > 1)
        keep = 2 if number < layers_of_block - 2 else 1
        *states, sums = run(number, states, *norms, totals, kind="plain", keep=keep)
    far_lower = lax.ppermute(near_lower, "batch", cores)
    early, forcing, *sent = run(
        layers_of_block - 1,
        states[:1],
        *norms,
        gathered(sums, True, True),
        kind="last",
        extra=(coarse_begin, terms),
        cut=start,
    )
    kernels = call(
        gather_kernel,
        (weights, near_upper, near_lower, far_upper, far_lower),
        jax.ShapeDtypeStruct((2, 3, 3 * channels, channels), jnp.bfloat16),
        moved=9 * channels * channels * 8,
    )

    exchange = [lax.ppermute(part, "depth", partners) for part in sent]
    passed = [
        call(
            functools.partial(relay_kernel, low, high),
            (part, early),
            f32(half, high - low, width, channels),
            moved=half * (high - low) * width * channels * 8,
        )
        for part, (low, high) in zip(exchange, spans(start, rows))
    ]
    own = jnp.zeros((half, rows, width, channels), jnp.float32)
    gives = {
        (low, high): jnp.zeros((half, high - low, width, channels), jnp.float32)
        for low, high in spans(plan[-1][2], rows)
    }
    back_spans = list(gives)
    back = []
    shared = (forcing, terms, kernels)
    for turn, (cuts, split, out_cuts) in enumerate(plan, 1):
        across = {2 * turn - 2: 2 * turn, 2 * turn - 1: 2 * turn + 1}
        across.update({b: a for a, b in across.items()})
        route = [(i, across.get(i, i ^ 1)) for i in range(devices)]
        arriving = [lax.ppermute(part, "depth", route) for part in passed]
        last = turn == len(plan)
        if not split:
            passed, own, gives = pair(
                turn, None, cuts, start, out_cuts, last, arriving, exchange, shared, own, gives
            )
            continue
        passed, halo = [], ()
        for n in range(len(cuts) + 1):
            incoming = (*arriving[max(n - 1, 0) : n + 1], *halo)
            now = {span: gives[span] for span in back_spans[n : n + 2]} if last else gives
            made, own, now = pair(
                turn,
                n,
                cuts,
                start,
                out_cuts,
                last,
                incoming,
                exchange[: n + 1],
                shared,
                own,
                now,
            )
            gives = {**gives, **now}
            halo = tuple(made[:1]) if n < len(cuts) else ()
            if last:
                back.append(lax.ppermute(gives[back_spans[n]], "depth", partners))
            else:
                passed.append(made[-1])
    if not back:
        back = [lax.ppermute(part, "depth", partners) for part in gives.values()]
    out = call(
        finish_own_kernel,
        (early, own),
        f32(*initial.shape),
        [pltpu.SemaphoreType.DMA],
        out_specs=in_place,
        moved=initial.size * 8,
    )
    out = call(
        functools.partial(finish_kernel, plan[-1][2]),
        (*back, out),
        f32(*initial.shape),
        [pltpu.SemaphoreType.DMA((len(back),))],
        specs=[whole] * len(back) + [in_place],
        out_specs=in_place,
        aliases={len(back): 0},
        moved=initial.size * 4,
    )
    return out[None]


def solution(mesh):
    return jax.shard_map(
        steps,
        mesh=mesh,
        in_specs=(
            P("depth", "batch", None, None, None),
            P("depth", None, None, None, None),
            P("depth", None),
            P("depth", None),
        ),
        out_specs=P("depth", "batch", None, None, None),
        check_vma=False,
    )
```

```python
import functools
import jax
import jax.numpy as jnp
from jax import lax
from jax.experimental import pallas as pl
from jax.experimental.pallas import tpu as pltpu
from jax.sharding import PartitionSpec as P

fine_step = 0.125
coarse_step = 0.5
epsilon = 1e-05
layers_of_block = 4
vmem_bytes = 16 << 20


whole = pl.BlockSpec(memory_space=pltpu.VMEM)
in_place = pl.BlockSpec(memory_space=pltpu.HBM)


def call(
    body, operands, outs, scratch=(), specs=None, out_specs=None, aliases=None,
    flops=0, moved=0, limit=vmem_bytes,
):
    return pl.pallas_call(
        body,
        out_shape=outs,
        in_specs=[whole] * len(operands) if specs is None else specs,
        out_specs=jax.tree.map(lambda _: whole, outs) if out_specs is None else out_specs,
        scratch_shapes=list(scratch),
        input_output_aliases=aliases or {},
        compiler_params=pltpu.CompilerParams(vmem_limit_bytes=limit),
        cost_estimate=pl.CostEstimate(flops=flops, bytes_accessed=moved, transcendentals=0),
    )(*operands)


def f32(*shape):
    return jax.ShapeDtypeStruct(shape, jnp.float32)


def lay_out(activated, taps, width, above=True, below=True):
    entries, channels = activated.shape
    column = lax.broadcasted_iota(jnp.int32, (entries, 1), 0) % width
    before = jnp.where(column == 0, 0.0, pltpu.roll(activated, 1, 0))
    after = jnp.where(column == width - 1, 0.0, pltpu.roll(activated, entries - 1, 0))
    edge = jnp.zeros((width, 3 * channels), jnp.bfloat16)
    start = width if above else 0
    if above:
        taps[0:width] = edge
    if below:
        taps[start + entries : start + entries + width] = edge
    for place, values in enumerate((before, activated, after)):
        taps[start : start + entries, place * channels : (place + 1) * channels] = values.astype(
            jnp.bfloat16
        )


def convolved(taps, kernel, width, entries):
    total = jnp.dot(taps[0:entries], kernel(0), preferred_element_type=jnp.float32)
    for row in (1, 2):
        total += jnp.dot(
            taps[row * width : row * width + entries],
            kernel(row),
            preferred_element_type=jnp.float32,
        )
    return total


def both_sums(values):
    return jnp.concatenate(
        [jnp.sum(values, axis=0, keepdims=True), jnp.sum(values * values, axis=0, keepdims=True)],
        axis=0,
    )


def spans(cuts, rows):
    edges = (0, *cuts, rows)
    return list(zip(edges, edges[1:]))


def sums_kernel(state, held, sums):
    samples, rows, width, channels = state.shape
    total = jnp.zeros((2, channels), jnp.float32)
    for i in range(samples):
        held[i] = state[i]
        total += both_sums(state[i].reshape(rows * width, channels))
    sums[...] = total


def copy_kernel(*refs):
    refs[-1][...] = refs[0][...]


def statistics(totals, entries):
    center = totals[0:1] * (1.0 / entries)
    return center, lax.rsqrt(totals[1:2] * (1.0 / entries) - center * center + epsilon)


def layer_kernel(number, count, keep, parts, batch_entries, kind, cut, *refs):
    states, refs = refs[:count], refs[count:]
    weights, gains, offsets = refs[:3]
    totals = refs[3 : 3 + parts]
    refs = refs[3 + parts :]
    position = lax.axis_index("depth")
    if kind == "first":
        initial, initial_totals = refs[0], refs[1 : 1 + lax.axis_size("batch")]
        outs, taps = refs[1 + len(initial_totals) : -1], refs[-1]
    elif kind == "last":
        coarse_begin, terms = refs[:2]
        outs, taps, kept_forcing = refs[2:-2], refs[-2], refs[-1]
    else:
        outs, taps = refs[:-1], refs[-1]
    samples, rows, width, channels = states[0].shape
    entries = rows * width

    def load(i):
        values = states[i // samples][i % samples]
        if kind == "first":
            values = jnp.where(position == 0, initial[i], values)
        return values.reshape(entries, channels)

    def added(pieces):
        summed = pieces[0][...]
        for piece in pieces[1:]:
            summed = summed + piece[...]
        return summed

    summed = added(totals)
    if kind == "first":
        summed = jnp.where(position == 0, added(initial_totals), summed)
    center, inverse = statistics(summed, batch_entries)
    scale = gains[number : number + 1] * inverse
    offset = offsets[number : number + 1]
    for i in range(count * samples):
        lay_out(jnp.maximum((load(i) - center) * scale + offset, 0.0), taps.at[i], width)
    total = jnp.zeros((2, channels), jnp.float32)
    for i in range(count * samples):
        change = convolved(taps.at[i], lambda row: weights[number, row], width, entries)
        values = load(i)
        made = values + fine_step * change
        if kind == "last":
            begun = coarse_begin[i].reshape(entries, channels)
            forcing = made - begun
            outs[0][i] = (begun + forcing).reshape(rows, width, channels)
            kept_forcing[i] = forcing
        else:
            if i < keep * samples:
                outs[i // samples][i % samples] = made.reshape(rows, width, channels)
            total += both_sums(made)
            if kind == "first":
                outs[2][i] = (values + coarse_step * change).reshape(rows, width, channels)
    if kind == "last":
        half = samples // 2
        other = (1 - position % 2) * half
        for i in range(half):
            outs[1][i] = kept_forcing[position % 2 * half + i]
            sent = jnp.where(
                position == 1, outs[0][other + i].reshape(entries, channels), kept_forcing[other + i]
            )
            for (low, high), out in zip(spans(cut, rows), outs[2:]):
                size = (high - low) * width
                out[i * size : (i + 1) * size] = sent[low * width : high * width]
        outs[2][half * cut[0] * width :] = terms[...]
    else:
        outs[keep][...] = total
    if kind == "first":
        outs[3][...] = jnp.concatenate(
            [center, scale, offset, jnp.zeros((5, channels), jnp.float32)], axis=0
        )


def layer(number, states, weights, gains, offsets, totals, batch_entries, kind, extra=(), cut=None, keep=None):
    state, keep = states[0], keep or len(states)
    samples, rows, width, channels = state.shape
    entries = rows * width
    half = samples // 2
    if kind == "last":
        outs = (
            f32(*state.shape),
            f32(half, entries, channels),
            *(
                f32(half * (high - low) * width + (8 if low == 0 else 0), channels)
                for low, high in spans(cut, rows)
            ),
        )
    else:
        outs = (*(f32(*state.shape) for state in states[:keep]), f32(2, channels))
        if kind == "first":
            outs += (f32(*state.shape), f32(8, channels))
    return call(
        functools.partial(
            layer_kernel, number, len(states), keep, len(totals), batch_entries, kind, cut
        ),
        (*states, weights, gains, offsets, *totals, *extra),
        outs,
        [pltpu.VMEM((len(states) * samples, entries + 2 * width, 3 * channels), jnp.bfloat16)]
        + ([pltpu.VMEM((samples, entries, channels), jnp.float32)] if kind == "last" else []),
        flops=2 * len(states) * samples * entries * 9 * channels * channels,
        moved=4 * len(states) * samples * entries * channels,
    )


def widen_kernel(part, weights, after, out):
    piece = out.shape[0] // 3
    at = pl.multiple_of((lax.axis_index("batch") % 2) * 2 * piece + part * piece, piece)
    for row in range(3):
        out[row * piece : (row + 1) * piece] = weights[0, row, pl.ds(at, piece)].astype(jnp.float32)


def widen(part, weights, after):
    inner, channels = weights.shape[2:]
    piece = inner // 4
    return call(
        functools.partial(widen_kernel, part),
        (weights, after),
        f32(3 * piece, channels),
        moved=3 * piece * channels * 6,
    )


def stage_kernel(weights, out, done):
    copies = [
        pltpu.make_async_copy(weights.at[n], out.at[n], done.at[n]) for n in range(out.shape[0])
    ]
    for copy in copies:
        copy.start()
    for copy in copies:
        copy.wait()


def gather_kernel(weights, near_upper, near_lower, far_upper, far_lower, out):
    parity, core = lax.axis_index("depth") % 2, lax.axis_index("batch") % 2
    piece = near_upper.shape[0] // 3
    out[parity] = weights[0]
    for part, pieces in enumerate(((near_upper, far_upper), (near_lower, far_lower))):
        for owner, source in ((core, pieces[0]), (1 - core, pieces[1])):
            at = pl.multiple_of(owner * 2 * piece + part * piece, piece)
            for row in range(3):
                values = source[row * piece : (row + 1) * piece]
                out[1 - parity, row, pl.ds(at, piece)] = values.astype(jnp.bfloat16)


def relay_kernel(low, high, received, early, out):
    half, rows, width, channels = out.shape
    entries = rows * width
    odd = lax.axis_index("depth") % 2 == 1
    for i in range(half):
        passed = received[i * entries : (i + 1) * entries].reshape(rows, width, channels)
        out[i] = jnp.where(odd, early[half + i, low:high], passed)


def pair_kernel(turn, piece, cuts, start_cuts, kept, out_cuts, last, *refs):
    refs, taps = list(refs[:-1]), refs[-1]
    take = lambda count: [refs.pop(0) for _ in range(count)]
    pieces = len(cuts) + 1
    is_last = piece is None or piece == pieces - 1
    if piece is None:
        incoming, halo = take(pieces), []
    elif piece == 0:
        incoming, halo = take(1), []
    else:
        incoming, halo = take(2), take(1)
    exchange = take(pieces if piece is None else piece + 1)
    forcing, terms, kernels = take(3)
    take(1 + len(kept))
    gives = {low_high: ref for low_high, ref in zip(kept, refs[len(refs) - len(kept) :])}
    own = refs[len(refs) - len(kept) - 1]
    made = refs[: len(refs) - len(kept) - 1]
    half, height, width, channels = own.shape
    position = lax.axis_index("depth")
    parity = position % 2

    def flat(values):
        return values.reshape(-1, channels)

    def joined(values):
        return values[0] if len(values) == 1 else jnp.concatenate(values, axis=0)

    def forced(stage, i, low, high):
        here = forcing[i, low * width : high * width]
        there = []
        for (first, end), ref in zip(spans(start_cuts, height), exchange):
            a, b = max(low, first), min(high, end)
            if a < b:
                base = i * (end - first) - first
                there.append(ref[(base + a) * width : (base + b) * width])
        return jnp.where(parity == stage, here, joined(there))

    def mapped(stage, i, values, begin, low, high):
        base = half * start_cuts[0] * width
        center, scale, offset = (
            jnp.where(parity == stage, terms[n : n + 1], exchange[0][base + n : base + n + 1])
            for n in range(3)
        )
        lay_out(
            jnp.maximum((values - center) * scale + offset, 0.0),
            taps.at[i, stage],
            width,
            low == 0,
            high == height,
        )
        change = convolved(
            taps.at[i, stage], lambda row: kernels[stage, row], width, (high - low) * width
        )
        kept_values = values[(low - begin) * width : (high - begin) * width]
        return kept_values + coarse_step * change + forced(stage, i, low, high)

    def put(i, low, values, is_own):
        high = low + values.shape[0] // width
        values = values.reshape(high - low, width, channels)
        if is_own:
            own[i, low:high] = values
            return
        for (first, end), ref in gives.items():
            a, b = max(low, first), min(high, end)
            if a < b:
                ref[i, a - first : b - first] = values[a - low : b - low]

    @pl.when(position // 2 == turn)
    def _():
        for i in range(half):
            if halo:
                cut = cuts[piece - 1]
                low = (cut - 1, cut - 2)
                values = joined([flat(incoming[0][i, -2:]), flat(incoming[1][i])])
                begin = (cut - 2, cut - 3)
            else:
                low, begin = (0, 0), (0, 0)
                values = joined([flat(part[i]) for part in incoming])
            high = (height, height) if is_last else (cuts[piece] - 1, cuts[piece] - 2)
            first = mapped(0, i, values, begin[0], low[0], high[0])
            values = joined([flat(halo[0][i, -2:]), first]) if halo else first
            second = mapped(1, i, values, begin[1], low[1], high[1])
            outs = list(made)
            if not is_last:
                outs.pop(0)[i] = first.reshape(-1, width, channels)
            if not last:
                for a, b in spans(out_cuts, height) if piece is None else [(low[1], high[1])]:
                    at = slice((a - low[1]) * width, (b - low[1]) * width)
                    outs.pop(0)[i] = second[at].reshape(-1, width, channels)

            @pl.when(parity == 0)
            def _():
                put(i, low[0], first, True)
                put(i, low[1], second, False)

            @pl.when(parity == 1)
            def _():
                put(i, low[0], first, False)
                put(i, low[1], second, True)


def pair(turn, piece, cuts, start_cuts, out_cuts, last, incoming, exchange, shared, own, gives):
    half, height, width, channels = own.shape
    pieces = len(cuts) + 1
    is_last = piece is None or piece == pieces - 1
    rows = lambda low, high: f32(half, high - low, width, channels)
    made = []
    if not is_last:
        low = cuts[piece - 1] - 1 if piece else 0
        made.append(rows(low, cuts[piece] - 1))
    if not last:
        if piece is None:
            made += [rows(*span) for span in spans(out_cuts, height)]
        else:
            made.append(rows(*spans(out_cuts, height)[piece]))
    kept = tuple(gives)
    carried = (own, *gives.values())
    operands = (*incoming, *exchange, *shared, *carried)
    count = len(operands) - len(carried)
    entries = half * height * width // pieces
    outs = call(
        functools.partial(pair_kernel, turn, piece, cuts, start_cuts, kept, out_cuts, last),
        operands,
        tuple(made) + tuple(f32(*part.shape) for part in carried),
        [pltpu.VMEM((half, 2, (height + 2) * width, 3 * channels), jnp.bfloat16)],
        aliases={count + n: len(made) + n for n in range(len(carried))},
        flops=4 * entries * 9 * channels * channels,
        moved=8 * entries * channels,
    )
    rest = outs[len(made) :]
    return outs[: len(made)], rest[0], dict(zip(kept, rest[1:]))


def finish_own_kernel(early, own, own_other, out, done):
    half = own.shape[0]
    position = lax.axis_index("depth")
    here = out.at[pl.ds((position % 2) * half, half)]
    for condition, source, target in (
        (position < 2, early, out),
        ((position >= 2) & (position // 2 % 2 == 0), own, here),
        (position // 2 % 2 == 1, own_other, here),
    ):

        @pl.when(condition)
        def _(source=source, target=target):
            copy = pltpu.make_async_copy(source, target, done)
            copy.start()
            copy.wait()


def finish_kernel(cuts, *refs):
    pieces, out, done = refs[: len(cuts) + 1], refs[-2], refs[-1]
    half = pieces[0].shape[0]
    position = lax.axis_index("depth")

    @pl.when(position >= 2)
    def _():
        there = pl.ds((1 - position % 2) * half, half)
        copies = [
            pltpu.make_async_copy(piece, out.at[there, low:high], done.at[n])
            for n, (piece, (low, high)) in enumerate(zip(pieces, spans(cuts, out.shape[1])))
        ]
        for copy in copies:
            copy.start()
        for copy in copies:
            copy.wait()


def turns_of(count, height):
    start = (height // 2, height * 7 // 8)
    plan, cuts = [], start
    for _ in range(count):
        split = cuts[0] >= 3
        plan.append((cuts, split, tuple(cut - 2 for cut in cuts) if split else start))
        cuts = plan[-1][2]
    return start, plan


def steps(iterate, weights, norm_scale, norm_shift):
    initial = iterate[0]
    samples, rows, width, channels = initial.shape
    half = samples // 2
    devices = lax.axis_size("depth")
    group = lax.axis_size("batch")
    batch_entries = samples * rows * width * group
    weights = weights.reshape(layers_of_block, 3, 3 * channels, channels)
    run = functools.partial(layer, batch_entries=batch_entries)

    def gathered(sums, mark=False, chips=False, ready=()):
        others = [
            lax.ppermute(sums, "batch", [(i, i ^ m) for i in range(group)])
            for m in (range(3, group, 2) if chips else range(1, group))
        ]
        if mark:
            sums = call(copy_kernel, (sums, *ready), f32(*sums.shape))
        return (sums, *others)

    both = ("depth", "batch")

    def routes(of):
        return [
            (i * group + b, of(i)[0] * group + (b ^ 1 if of(i)[1] else b))
            for i in range(devices)
            for b in range(group)
        ]

    swaps = routes(lambda i: (i ^ 1, i // 2 % 2 == 1))
    partners = [(i, i ^ 1) for i in range(devices)]
    cores = [(i, i ^ 1) for i in range(group)]
    onward = [(i, i + 1) for i in range(devices - 1)]

    initial, sums = call(
        sums_kernel, (initial,), (f32(*initial.shape), f32(2, channels)), moved=initial.size * 4
    )
    first_totals = gathered(sums)
    other = lax.ppermute(initial, "batch", cores)
    weights = call(
        stage_kernel,
        (weights,),
        jax.ShapeDtypeStruct(weights.shape, weights.dtype),
        [pltpu.SemaphoreType.DMA((layers_of_block,))],
        specs=[in_place],
        moved=weights.size * 4,
        limit=47 << 20,
    )
    norms = (weights, norm_scale, norm_shift)
    states, totals = (initial, other), first_totals
    for number in range(layers_of_block - 1):
        keep = 2 if number < layers_of_block - 2 else 1
        *states, sums = run(number, states, *norms, totals, kind="plain", keep=keep)
        if number == 0:
            near_upper = lax.ppermute(widen(0, weights, sums), "depth", partners)
        totals = gathered(sums, number == 0, True)
    current, sums = run(layers_of_block - 1, states[:1], *norms, totals, kind="plain")
    totals = gathered(sums)
    arrived = lax.ppermute(current, "depth", onward)
    arrived_totals = lax.ppermute(sum(totals[1:], totals[0]), "depth", onward)

    start, plan = turns_of(devices // 2 - 1, rows)
    current, sums, coarse_begin, terms = run(
        0, (arrived,), *norms, (arrived_totals,), kind="first", extra=(initial, *first_totals)
    )
    other = lax.ppermute(current, "batch", cores)
    near_lower = lax.ppermute(widen(1, weights, sums), "depth", partners)
    far_upper = lax.ppermute(near_upper, "batch", cores)
    states = (current, other)
    for number in range(1, layers_of_block - 1):
        totals = gathered(sums, number == 1, number > 1)
        keep = 2 if number < layers_of_block - 2 else 1
        *states, sums = run(number, states, *norms, totals, kind="plain", keep=keep)
    far_lower = lax.ppermute(near_lower, "batch", cores)
    early, mine, *sent = run(
        layers_of_block - 1,
        states[:1],
        *norms,
        gathered(sums, True, True),
        kind="last",
        extra=(coarse_begin, terms),
        cut=start,
    )
    kernels = call(
        gather_kernel,
        (weights, near_upper, near_lower, far_upper, far_lower),
        jax.ShapeDtypeStruct((2, 3, 3 * channels, channels), jnp.bfloat16),
        moved=9 * channels * channels * 8,
    )

    exchange = [lax.ppermute(part, both, swaps) for part in sent]
    mine_other = lax.ppermute(mine, "batch", cores)
    passed = [
        call(
            functools.partial(relay_kernel, low, high),
            (part, early),
            f32(half, high - low, width, channels),
            moved=half * (high - low) * width * channels * 8,
        )
        for part, (low, high) in zip(exchange, spans(start, rows))
    ]
    own = jnp.zeros((half, rows, width, channels), jnp.float32)
    gives = {
        (low, high): jnp.zeros((half, high - low, width, channels), jnp.float32)
        for low, high in spans(plan[-1][2], rows)
    }
    back_spans = list(gives)
    back = []
    for turn, (cuts, split, out_cuts) in enumerate(plan, 1):
        across = {}
        for first in (turn - 1, *range(0, turn - 2, 2), *range(turn + 1, devices // 2 - 1, 2)):
            for i in (2 * first, 2 * first + 1):
                across[i], across[i + 2] = (i + 2, first == turn - 1), (i, first == turn - 1)
        route = routes(lambda i: across.get(i, (i ^ 1, False)))
        arriving = [lax.ppermute(part, both, route) for part in passed]
        shared = (mine_other if turn % 2 else mine, terms, kernels)
        last = turn == len(plan)
        if not split:
            passed, own, gives = pair(
                turn, None, cuts, start, out_cuts, last, arriving, exchange, shared, own, gives
            )
            continue
        passed, halo = [], ()
        for n in range(len(cuts) + 1):
            incoming = (*arriving[max(n - 1, 0) : n + 1], *halo)
            now = {span: gives[span] for span in back_spans[n : n + 2]} if last else gives
            made, own, now = pair(
                turn,
                n,
                cuts,
                start,
                out_cuts,
                last,
                incoming,
                exchange[: n + 1],
                shared,
                own,
                now,
            )
            gives = {**gives, **now}
            halo = tuple(made[:1]) if n < len(cuts) else ()
            if last:
                back.append(lax.ppermute(gives[back_spans[n]], both, swaps))
            else:
                passed.append(made[-1])
    if not back:
        back = [lax.ppermute(part, both, swaps) for part in gives.values()]
    out = call(
        finish_own_kernel,
        (early, own, lax.ppermute(own, "batch", cores)),
        f32(*initial.shape),
        [pltpu.SemaphoreType.DMA],
        out_specs=in_place,
        moved=initial.size * 8,
    )
    out = call(
        functools.partial(finish_kernel, plan[-1][2]),
        (*back, out),
        f32(*initial.shape),
        [pltpu.SemaphoreType.DMA((len(back),))],
        specs=[whole] * len(back) + [in_place],
        out_specs=in_place,
        aliases={len(back): 0},
        moved=initial.size * 4,
    )
    return out[None]


def solution(mesh):
    return jax.shard_map(
        steps,
        mesh=mesh,
        in_specs=(
            P("depth", "batch", None, None, None),
            P("depth", None, None, None, None),
            P("depth", None),
            P("depth", None),
        ),
        out_specs=P("depth", "batch", None, None, None),
        check_vma=False,
    )
```

```python
import functools
import jax
import jax.numpy as jnp
from jax import lax
from jax.experimental import pallas as pl
from jax.experimental.pallas import tpu as pltpu
from jax.sharding import PartitionSpec as P

fine_step = 0.125
coarse_step = 0.5
epsilon = 1e-05
layers_of_block = 4
vmem_bytes = 16 << 20


whole = pl.BlockSpec(memory_space=pltpu.VMEM)
in_place = pl.BlockSpec(memory_space=pltpu.HBM)


def call(
    body, operands, outs, scratch=(), specs=None, out_specs=None, aliases=None,
    flops=0, moved=0, limit=vmem_bytes,
):
    return pl.pallas_call(
        body,
        out_shape=outs,
        in_specs=[whole] * len(operands) if specs is None else specs,
        out_specs=jax.tree.map(lambda _: whole, outs) if out_specs is None else out_specs,
        scratch_shapes=list(scratch),
        input_output_aliases=aliases or {},
        compiler_params=pltpu.CompilerParams(vmem_limit_bytes=limit),
        cost_estimate=pl.CostEstimate(flops=flops, bytes_accessed=moved, transcendentals=0),
    )(*operands)


def f32(*shape):
    return jax.ShapeDtypeStruct(shape, jnp.float32)


def lay_out(activated, taps, width, above=True, below=True):
    entries, channels = activated.shape
    column = lax.broadcasted_iota(jnp.int32, (entries, 1), 0) % width
    before = jnp.where(column == 0, 0.0, pltpu.roll(activated, 1, 0))
    after = jnp.where(column == width - 1, 0.0, pltpu.roll(activated, entries - 1, 0))
    edge = jnp.zeros((width, 3 * channels), jnp.bfloat16)
    start = width if above else 0
    if above:
        taps[0:width] = edge
    if below:
        taps[start + entries : start + entries + width] = edge
    for place, values in enumerate((before, activated, after)):
        taps[start : start + entries, place * channels : (place + 1) * channels] = values.astype(
            jnp.bfloat16
        )


def convolved(taps, kernel, width, entries):
    total = jnp.dot(taps[0:entries], kernel(0), preferred_element_type=jnp.float32)
    for row in (1, 2):
        total += jnp.dot(
            taps[row * width : row * width + entries],
            kernel(row),
            preferred_element_type=jnp.float32,
        )
    return total


def both_sums(values):
    return jnp.concatenate(
        [jnp.sum(values, axis=0, keepdims=True), jnp.sum(values * values, axis=0, keepdims=True)],
        axis=0,
    )


def spans(cuts, rows):
    edges = (0, *cuts, rows)
    return list(zip(edges, edges[1:]))


def sums_kernel(state, held, sums):
    samples, rows, width, channels = state.shape
    total = jnp.zeros((2, channels), jnp.float32)
    for i in range(samples):
        held[i] = state[i]
        total += both_sums(state[i].reshape(rows * width, channels))
    sums[...] = total


def copy_kernel(*refs):
    refs[-1][...] = refs[0][...]


def statistics(totals, entries):
    center = totals[0:1] * (1.0 / entries)
    return center, lax.rsqrt(totals[1:2] * (1.0 / entries) - center * center + epsilon)


def layer_kernel(number, count, keep, parts, batch_entries, kind, cut, *refs):
    states, refs = refs[:count], refs[count:]
    weights, gains, offsets = refs[:3]
    totals = refs[3 : 3 + parts]
    refs = refs[3 + parts :]
    position = lax.axis_index("depth")
    if kind == "first":
        initial, initial_totals = refs[0], refs[1 : 1 + lax.axis_size("batch")]
        outs, taps = refs[1 + len(initial_totals) : -1], refs[-1]
    elif kind == "last":
        coarse_begin, terms = refs[:2]
        outs, taps, kept_forcing = refs[2:-2], refs[-2], refs[-1]
    else:
        outs, taps = refs[:-1], refs[-1]
    samples, rows, width, channels = states[0].shape
    entries = rows * width

    def load(i):
        values = states[i // samples][i % samples]
        if kind == "first":
            values = jnp.where(position == 0, initial[i], values)
        return values.reshape(entries, channels)

    def added(pieces):
        summed = pieces[0][...]
        for piece in pieces[1:]:
            summed = summed + piece[...]
        return summed

    summed = added(totals)
    if kind == "first":
        summed = jnp.where(position == 0, added(initial_totals), summed)
    center, inverse = statistics(summed, batch_entries)
    scale = gains[number : number + 1] * inverse
    offset = offsets[number : number + 1]
    for i in range(count * samples):
        lay_out(jnp.maximum((load(i) - center) * scale + offset, 0.0), taps.at[i], width)
    total = jnp.zeros((2, channels), jnp.float32)
    for i in range(count * samples):
        change = convolved(taps.at[i], lambda row: weights[number, row], width, entries)
        values = load(i)
        made = values + fine_step * change
        if kind == "last":
            begun = coarse_begin[i].reshape(entries, channels)
            forcing = made - begun
            outs[0][i] = (begun + forcing).reshape(rows, width, channels)
            kept_forcing[i] = forcing
        else:
            if i < keep * samples:
                outs[i // samples][i % samples] = made.reshape(rows, width, channels)
            total += both_sums(made)
            if kind == "first":
                outs[2][i] = (values + coarse_step * change).reshape(rows, width, channels)
    if kind == "last":
        half = samples // 2
        other = (1 - position % 2) * half
        for i in range(half):
            outs[1][i] = kept_forcing[position % 2 * half + i]
            sent = jnp.where(
                position == 1, outs[0][other + i].reshape(entries, channels), kept_forcing[other + i]
            )
            for (low, high), out in zip(spans(cut, rows), outs[2:]):
                size = (high - low) * width
                out[i * size : (i + 1) * size] = sent[low * width : high * width]
        outs[2][half * cut[0] * width :] = terms[...]
    else:
        outs[keep][...] = total
    if kind == "first":
        outs[3][...] = jnp.concatenate(
            [center, scale, offset, jnp.zeros((5, channels), jnp.float32)], axis=0
        )


def layer(number, states, weights, gains, offsets, totals, batch_entries, kind, extra=(), cut=None, keep=None):
    state, keep = states[0], keep or len(states)
    samples, rows, width, channels = state.shape
    entries = rows * width
    half = samples // 2
    if kind == "last":
        outs = (
            f32(*state.shape),
            f32(half, entries, channels),
            *(
                f32(half * (high - low) * width + (8 if low == 0 else 0), channels)
                for low, high in spans(cut, rows)
            ),
        )
    else:
        outs = (*(f32(*state.shape) for state in states[:keep]), f32(2, channels))
        if kind == "first":
            outs += (f32(*state.shape), f32(8, channels))
    return call(
        functools.partial(
            layer_kernel, number, len(states), keep, len(totals), batch_entries, kind, cut
        ),
        (*states, weights, gains, offsets, *totals, *extra),
        outs,
        [pltpu.VMEM((len(states) * samples, entries + 2 * width, 3 * channels), jnp.bfloat16)]
        + ([pltpu.VMEM((samples, entries, channels), jnp.float32)] if kind == "last" else []),
        flops=2 * len(states) * samples * entries * 9 * channels * channels,
        moved=4 * len(states) * samples * entries * channels,
    )


def widen_kernel(part, weights, after, out):
    piece = out.shape[0] // 3
    at = pl.multiple_of((lax.axis_index("batch") % 2) * 2 * piece + part * piece, piece)
    for row in range(3):
        out[row * piece : (row + 1) * piece] = weights[0, row, pl.ds(at, piece)].astype(jnp.float32)


def widen(part, weights, after):
    inner, channels = weights.shape[2:]
    piece = inner // 4
    return call(
        functools.partial(widen_kernel, part),
        (weights, after),
        f32(3 * piece, channels),
        moved=3 * piece * channels * 6,
    )


def stage_kernel(weights, out, done):
    copies = [
        pltpu.make_async_copy(weights.at[n], out.at[n], done.at[n]) for n in range(out.shape[0])
    ]
    for copy in copies:
        copy.start()
    for copy in copies:
        copy.wait()


def gather_kernel(weights, near_upper, near_lower, far_upper, far_lower, out):
    parity, core = lax.axis_index("depth") % 2, lax.axis_index("batch") % 2
    piece = near_upper.shape[0] // 3
    out[parity] = weights[0]
    for part, pieces in enumerate(((near_upper, far_upper), (near_lower, far_lower))):
        for owner, source in ((core, pieces[0]), (1 - core, pieces[1])):
            at = pl.multiple_of(owner * 2 * piece + part * piece, piece)
            for row in range(3):
                values = source[row * piece : (row + 1) * piece]
                out[1 - parity, row, pl.ds(at, piece)] = values.astype(jnp.bfloat16)


def relay_kernel(low, high, received, early, out):
    half, rows, width, channels = out.shape
    entries = rows * width
    odd = lax.axis_index("depth") % 2 == 1
    for i in range(half):
        passed = received[i * entries : (i + 1) * entries].reshape(rows, width, channels)
        out[i] = jnp.where(odd, early[half + i, low:high], passed)


def pair_kernel(turn, piece, cuts, start_cuts, kept, out_cuts, last, *refs):
    refs, taps = list(refs[:-1]), refs[-1]
    take = lambda count: [refs.pop(0) for _ in range(count)]
    pieces = len(cuts) + 1
    is_last = piece is None or piece == pieces - 1
    if piece is None:
        incoming, halo = take(pieces), []
    elif piece == 0:
        incoming, halo = take(1), []
    else:
        incoming, halo = take(2), take(1)
    exchange = take(pieces if piece is None else piece + 1)
    forcing, terms, kernels = take(3)
    take(1 + len(kept))
    gives = {low_high: ref for low_high, ref in zip(kept, refs[len(refs) - len(kept) :])}
    own = refs[len(refs) - len(kept) - 1]
    made = refs[: len(refs) - len(kept) - 1]
    half, height, width, channels = own.shape
    position = lax.axis_index("depth")
    parity = position % 2

    def flat(values):
        return values.reshape(-1, channels)

    def joined(values):
        return values[0] if len(values) == 1 else jnp.concatenate(values, axis=0)

    def forced(stage, i, low, high):
        here = forcing[i, low * width : high * width]
        there = []
        for (first, end), ref in zip(spans(start_cuts, height), exchange):
            a, b = max(low, first), min(high, end)
            if a < b:
                base = i * (end - first) - first
                there.append(ref[(base + a) * width : (base + b) * width])
        return jnp.where(parity == stage, here, joined(there))

    def mapped(stage, i, values, begin, low, high):
        base = half * start_cuts[0] * width
        center, scale, offset = (
            jnp.where(parity == stage, terms[n : n + 1], exchange[0][base + n : base + n + 1])
            for n in range(3)
        )
        lay_out(
            jnp.maximum((values - center) * scale + offset, 0.0),
            taps.at[i, stage],
            width,
            low == 0,
            high == height,
        )
        change = convolved(
            taps.at[i, stage], lambda row: kernels[stage, row], width, (high - low) * width
        )
        kept_values = values[(low - begin) * width : (high - begin) * width]
        return kept_values + coarse_step * change + forced(stage, i, low, high)

    def put(i, low, values, is_own):
        high = low + values.shape[0] // width
        values = values.reshape(high - low, width, channels)
        if is_own:
            own[i, low:high] = values
            return
        for (first, end), ref in gives.items():
            a, b = max(low, first), min(high, end)
            if a < b:
                ref[i, a - first : b - first] = values[a - low : b - low]

    @pl.when(position // 2 == turn)
    def _():
        for i in range(half):
            if halo:
                cut = cuts[piece - 1]
                low = (cut - 1, cut - 2)
                values = joined([flat(incoming[0][i, -2:]), flat(incoming[1][i])])
                begin = (cut - 2, cut - 3)
            else:
                low, begin = (0, 0), (0, 0)
                values = joined([flat(part[i]) for part in incoming])
            high = (height, height) if is_last else (cuts[piece] - 1, cuts[piece] - 2)
            first = mapped(0, i, values, begin[0], low[0], high[0])
            values = joined([flat(halo[0][i, -2:]), first]) if halo else first
            second = mapped(1, i, values, begin[1], low[1], high[1])
            outs = list(made)
            if not is_last:
                outs.pop(0)[i] = first.reshape(-1, width, channels)
            if not last:
                for a, b in spans(out_cuts, height) if piece is None else [(low[1], high[1])]:
                    at = slice((a - low[1]) * width, (b - low[1]) * width)
                    outs.pop(0)[i] = second[at].reshape(-1, width, channels)

            @pl.when(parity == 0)
            def _():
                put(i, low[0], first, True)
                put(i, low[1], second, False)

            @pl.when(parity == 1)
            def _():
                put(i, low[0], first, False)
                put(i, low[1], second, True)


def pair(turn, piece, cuts, start_cuts, out_cuts, last, incoming, exchange, shared, own, gives):
    half, height, width, channels = own.shape
    pieces = len(cuts) + 1
    is_last = piece is None or piece == pieces - 1
    rows = lambda low, high: f32(half, high - low, width, channels)
    made = []
    if not is_last:
        low = cuts[piece - 1] - 1 if piece else 0
        made.append(rows(low, cuts[piece] - 1))
    if not last:
        if piece is None:
            made += [rows(*span) for span in spans(out_cuts, height)]
        else:
            made.append(rows(*spans(out_cuts, height)[piece]))
    kept = tuple(gives)
    carried = (own, *gives.values())
    operands = (*incoming, *exchange, *shared, *carried)
    count = len(operands) - len(carried)
    entries = half * height * width // pieces
    outs = call(
        functools.partial(pair_kernel, turn, piece, cuts, start_cuts, kept, out_cuts, last),
        operands,
        tuple(made) + tuple(f32(*part.shape) for part in carried),
        [pltpu.VMEM((half, 2, (height + 2) * width, 3 * channels), jnp.bfloat16)],
        aliases={count + n: len(made) + n for n in range(len(carried))},
        flops=4 * entries * 9 * channels * channels,
        moved=8 * entries * channels,
    )
    rest = outs[len(made) :]
    return outs[: len(made)], rest[0], dict(zip(kept, rest[1:]))


def finish_own_kernel(early, own, own_other, out, done):
    half = own.shape[0]
    position = lax.axis_index("depth")
    here = out.at[pl.ds((position % 2) * half, half)]
    for condition, source, target in (
        (position < 2, early, out),
        ((position >= 2) & (position // 2 % 2 == 0), own, here),
        (position // 2 % 2 == 1, own_other, here),
    ):

        @pl.when(condition)
        def _(source=source, target=target):
            copy = pltpu.make_async_copy(source, target, done)
            copy.start()
            copy.wait()


def finish_kernel(cuts, *refs):
    pieces, out, done = refs[: len(cuts) + 1], refs[-2], refs[-1]
    half = pieces[0].shape[0]
    position = lax.axis_index("depth")

    @pl.when(position >= 2)
    def _():
        there = pl.ds((1 - position % 2) * half, half)
        copies = [
            pltpu.make_async_copy(piece, out.at[there, low:high], done.at[n])
            for n, (piece, (low, high)) in enumerate(zip(pieces, spans(cuts, out.shape[1])))
        ]
        for copy in copies:
            copy.start()
        for copy in copies:
            copy.wait()


def turns_of(count, height):
    start = (height // 2, height * 7 // 8)
    plan, cuts = [], start
    for _ in range(count):
        split = cuts[0] >= 3
        plan.append((cuts, split, tuple(cut - 2 for cut in cuts) if split else start))
        cuts = plan[-1][2]
    return start, plan


def steps(iterate, weights, norm_scale, norm_shift):
    initial = iterate[0]
    samples, rows, width, channels = initial.shape
    half = samples // 2
    devices = lax.axis_size("depth")
    group = lax.axis_size("batch")
    batch_entries = samples * rows * width * group
    weights = weights.reshape(layers_of_block, 3, 3 * channels, channels)
    run = functools.partial(layer, batch_entries=batch_entries)

    def gathered(sums, mark=False, chips=False, ready=()):
        others = [
            lax.ppermute(sums, "batch", [(i, i ^ m) for i in range(group)])
            for m in (range(3, group, 2) if chips else range(1, group))
        ]
        if mark:
            sums = call(copy_kernel, (sums, *ready), f32(*sums.shape))
        return (sums, *others)

    both = ("depth", "batch")

    def routes(of):
        return [
            (i * group + b, of(i)[0] * group + (b ^ 1 if of(i)[1] else b))
            for i in range(devices)
            for b in range(group)
        ]

    swaps = routes(lambda i: (i ^ 1, i // 2 % 2 == 1))
    backs = routes(lambda i: (i ^ 1, i // 2 % 2 == 1) if i > 1 else (i, True))
    partners = [(i, i ^ 1) for i in range(devices)]
    cores = [(i, i ^ 1) for i in range(group)]
    onward = [(i, i + 1) for i in range(devices - 1)]

    initial, sums = call(
        sums_kernel, (initial,), (f32(*initial.shape), f32(2, channels)), moved=initial.size * 4
    )
    first_totals = gathered(sums)
    other = lax.ppermute(initial, "batch", cores)
    weights = call(
        stage_kernel,
        (weights,),
        jax.ShapeDtypeStruct(weights.shape, weights.dtype),
        [pltpu.SemaphoreType.DMA((layers_of_block,))],
        specs=[in_place],
        moved=weights.size * 4,
        limit=47 << 20,
    )
    norms = (weights, norm_scale, norm_shift)
    states, totals = (initial, other), first_totals
    for number in range(layers_of_block - 1):
        keep = 2 if number < layers_of_block - 2 else 1
        *states, sums = run(number, states, *norms, totals, kind="plain", keep=keep)
        if number == 0:
            near_upper = lax.ppermute(widen(0, weights, sums), "depth", partners)
        totals = gathered(sums, number == 0, True)
    current, sums = run(layers_of_block - 1, states[:1], *norms, totals, kind="plain")
    totals = gathered(sums)
    arrived = lax.ppermute(current, "depth", onward)
    arrived_totals = lax.ppermute(sum(totals[1:], totals[0]), "depth", onward)

    start, plan = turns_of(devices // 2 - 1, rows)
    current, sums, coarse_begin, terms = run(
        0, (arrived,), *norms, (arrived_totals,), kind="first", extra=(initial, *first_totals)
    )
    other = lax.ppermute(current, "batch", cores)
    near_lower = lax.ppermute(widen(1, weights, sums), "depth", partners)
    far_upper = lax.ppermute(near_upper, "batch", cores)
    states = (current, other)
    for number in range(1, layers_of_block - 1):
        totals = gathered(sums, number == 1, number > 1)
        keep = 2 if number < layers_of_block - 2 else 1
        *states, sums = run(number, states, *norms, totals, kind="plain", keep=keep)
    far_lower = lax.ppermute(near_lower, "batch", cores)
    early, mine, *sent = run(
        layers_of_block - 1,
        states[:1],
        *norms,
        gathered(sums, True, True),
        kind="last",
        extra=(coarse_begin, terms),
        cut=start,
    )
    kernels = call(
        gather_kernel,
        (weights, near_upper, near_lower, far_upper, far_lower),
        jax.ShapeDtypeStruct((2, 3, 3 * channels, channels), jnp.bfloat16),
        moved=9 * channels * channels * 8,
    )

    exchange = [lax.ppermute(part, both, swaps) for part in sent]
    mine_other = lax.ppermute(mine, "batch", cores)
    passed = [
        call(
            functools.partial(relay_kernel, low, high),
            (part, early),
            f32(half, high - low, width, channels),
            moved=half * (high - low) * width * channels * 8,
        )
        for part, (low, high) in zip(exchange, spans(start, rows))
    ]
    own = jnp.zeros((half, rows, width, channels), jnp.float32)
    gives = {
        (low, high): jnp.zeros((half, high - low, width, channels), jnp.float32)
        for low, high in spans(plan[-1][2], rows)
    }
    back_spans = list(gives)
    back = []
    for turn, (cuts, split, out_cuts) in enumerate(plan, 1):
        across = {}
        for i in (2 * turn - 2, 2 * turn - 1):
            across[i], across[i + 2] = i + 2, i
        route = routes(lambda i: (across.get(i, i), True))
        arriving = [lax.ppermute(part, both, route) for part in passed]
        shared = (mine_other if turn % 2 else mine, terms, kernels)
        last = turn == len(plan)
        if not split:
            passed, own, gives = pair(
                turn, None, cuts, start, out_cuts, last, arriving, exchange, shared, own, gives
            )
            continue
        passed, halo = [], ()
        for n in range(len(cuts) + 1):
            incoming = (*arriving[max(n - 1, 0) : n + 1], *halo)
            now = {span: gives[span] for span in back_spans[n : n + 2]} if last else gives
            made, own, now = pair(
                turn,
                n,
                cuts,
                start,
                out_cuts,
                last,
                incoming,
                exchange[: n + 1],
                shared,
                own,
                now,
            )
            gives = {**gives, **now}
            halo = tuple(made[:1]) if n < len(cuts) else ()
            if last:
                back.append(lax.ppermute(gives[back_spans[n]], both, backs))
            else:
                passed.append(made[-1])
    if not back:
        back = [lax.ppermute(part, both, backs) for part in gives.values()]
    out = call(
        finish_own_kernel,
        (early, own, lax.ppermute(own, "batch", cores)),
        f32(*initial.shape),
        [pltpu.SemaphoreType.DMA],
        out_specs=in_place,
        moved=initial.size * 8,
    )
    out = call(
        functools.partial(finish_kernel, plan[-1][2]),
        (*back, out),
        f32(*initial.shape),
        [pltpu.SemaphoreType.DMA((len(back),))],
        specs=[whole] * len(back) + [in_place],
        out_specs=in_place,
        aliases={len(back): 0},
        moved=initial.size * 4,
    )
    return out[None]


def solution(mesh):
    return jax.shard_map(
        steps,
        mesh=mesh,
        in_specs=(
            P("depth", "batch", None, None, None),
            P("depth", None, None, None, None),
            P("depth", None),
            P("depth", None),
        ),
        out_specs=P("depth", "batch", None, None, None),
        check_vma=False,
    )
```

```python
import functools
import jax
import jax.numpy as jnp
from jax import lax
from jax.experimental import pallas as pl
from jax.experimental.pallas import tpu as pltpu
from jax.sharding import PartitionSpec as P

fine_step = 0.125
coarse_step = 0.5
epsilon = 1e-05
layers_of_block = 4
vmem_bytes = 16 << 20


whole = pl.BlockSpec(memory_space=pltpu.VMEM)
in_place = pl.BlockSpec(memory_space=pltpu.HBM)


def call(
    body, operands, outs, scratch=(), specs=None, out_specs=None, aliases=None,
    flops=0, moved=0, limit=vmem_bytes,
):
    return pl.pallas_call(
        body,
        out_shape=outs,
        in_specs=[whole] * len(operands) if specs is None else specs,
        out_specs=jax.tree.map(lambda _: whole, outs) if out_specs is None else out_specs,
        scratch_shapes=list(scratch),
        input_output_aliases=aliases or {},
        compiler_params=pltpu.CompilerParams(vmem_limit_bytes=limit),
        cost_estimate=pl.CostEstimate(flops=flops, bytes_accessed=moved, transcendentals=0),
    )(*operands)


def f32(*shape):
    return jax.ShapeDtypeStruct(shape, jnp.float32)


def lay_out(activated, taps, width, above=True, below=True):
    entries, channels = activated.shape
    column = lax.broadcasted_iota(jnp.int32, (entries, 1), 0) % width
    before = jnp.where(column == 0, 0.0, pltpu.roll(activated, 1, 0))
    after = jnp.where(column == width - 1, 0.0, pltpu.roll(activated, entries - 1, 0))
    edge = jnp.zeros((width, 3 * channels), jnp.bfloat16)
    start = width if above else 0
    if above:
        taps[0:width] = edge
    if below:
        taps[start + entries : start + entries + width] = edge
    for place, values in enumerate((before, activated, after)):
        taps[start : start + entries, place * channels : (place + 1) * channels] = values.astype(
            jnp.bfloat16
        )


def convolved(taps, kernel, width, entries):
    total = jnp.dot(taps[0:entries], kernel(0), preferred_element_type=jnp.float32)
    for row in (1, 2):
        total += jnp.dot(
            taps[row * width : row * width + entries],
            kernel(row),
            preferred_element_type=jnp.float32,
        )
    return total


def both_sums(values):
    return jnp.concatenate(
        [jnp.sum(values, axis=0, keepdims=True), jnp.sum(values * values, axis=0, keepdims=True)],
        axis=0,
    )


def spans(cuts, rows):
    edges = (0, *cuts, rows)
    return list(zip(edges, edges[1:]))


def sums_kernel(state, held, sums):
    samples, rows, width, channels = state.shape
    total = jnp.zeros((2, channels), jnp.float32)
    for i in range(samples):
        held[i] = state[i]
        total += both_sums(state[i].reshape(rows * width, channels))
    sums[...] = total


def copy_kernel(*refs):
    refs[-1][...] = refs[0][...]


def statistics(totals, entries):
    center = totals[0:1] * (1.0 / entries)
    return center, lax.rsqrt(totals[1:2] * (1.0 / entries) - center * center + epsilon)


def layer_kernel(number, slot, count, keep, parts, batch_entries, kind, cut, *refs):
    states, refs = refs[:count], refs[count:]
    weights, gains, offsets = refs[:3]
    totals = refs[3 : 3 + parts]
    refs = refs[3 + parts :]
    position = lax.axis_index("depth")
    if kind == "first":
        initial, initial_totals = refs[0], refs[1 : 1 + lax.axis_size("batch")]
        outs, taps = refs[1 + len(initial_totals) : -1], refs[-1]
    elif kind == "last":
        coarse_begin, terms = refs[:2]
        outs, taps, kept_forcing = refs[2:-2], refs[-2], refs[-1]
    else:
        outs, taps = refs[:-1], refs[-1]
    samples, rows, width, channels = states[0].shape
    entries = rows * width

    def load(i):
        values = states[i // samples][i % samples]
        if kind == "first":
            values = jnp.where(position == 0, initial[i], values)
        return values.reshape(entries, channels)

    def added(pieces):
        summed = pieces[0][...]
        for piece in pieces[1:]:
            summed = summed + piece[...]
        return summed

    summed = added(totals)
    if kind == "first":
        summed = jnp.where(position == 0, added(initial_totals), summed)
    center, inverse = statistics(summed, batch_entries)
    scale = gains[number : number + 1] * inverse
    offset = offsets[number : number + 1]
    for i in range(count * samples):
        lay_out(jnp.maximum((load(i) - center) * scale + offset, 0.0), taps.at[i], width)
    total = jnp.zeros((2, channels), jnp.float32)
    changes = 0.0
    for row in range(3):
        rows_in = [taps[i, row * width : row * width + entries] for i in range(count * samples)]
        changes += jnp.dot(
            jnp.concatenate(rows_in, axis=0), weights[slot, row], preferred_element_type=jnp.float32
        )
    for i in range(count * samples):
        change = changes[i * entries : (i + 1) * entries]
        values = load(i)
        made = values + fine_step * change
        if kind == "last":
            begun = coarse_begin[i].reshape(entries, channels)
            forcing = made - begun
            outs[0][i] = (begun + forcing).reshape(rows, width, channels)
            kept_forcing[i] = forcing
        else:
            if i < keep * samples:
                outs[i // samples][i % samples] = made.reshape(rows, width, channels)
            total += both_sums(made)
            if kind == "first":
                outs[2][i] = (values + coarse_step * change).reshape(rows, width, channels)
    if kind == "last":
        half = samples // 2
        other = (1 - position % 2) * half
        for i in range(half):
            outs[1][i] = kept_forcing[position % 2 * half + i]
            sent = jnp.where(
                position == 1, outs[0][other + i].reshape(entries, channels), kept_forcing[other + i]
            )
            for (low, high), out in zip(spans(cut, rows), outs[2:]):
                size = (high - low) * width
                out[i * size : (i + 1) * size] = sent[low * width : high * width]
        outs[2][half * cut[0] * width :] = terms[...]
    else:
        outs[keep][...] = total
    if kind == "first":
        outs[3][...] = jnp.concatenate(
            [center, scale, offset, jnp.zeros((5, channels), jnp.float32)], axis=0
        )


def layer(number, states, kernels, gains, offsets, totals, batch_entries, kind, extra=(), cut=None, keep=None):
    state, keep = states[0], keep or len(states)
    weights, slot = (kernels[0], 0) if number == 0 else (kernels[1], number - 1)
    samples, rows, width, channels = state.shape
    entries = rows * width
    half = samples // 2
    if kind == "last":
        outs = (
            f32(*state.shape),
            f32(half, entries, channels),
            *(
                f32(half * (high - low) * width + (8 if low == 0 else 0), channels)
                for low, high in spans(cut, rows)
            ),
        )
    else:
        outs = (*(f32(*state.shape) for state in states[:keep]), f32(2, channels))
        if kind == "first":
            outs += (f32(*state.shape), f32(8, channels))
    return call(
        functools.partial(
            layer_kernel, number, slot, len(states), keep, len(totals), batch_entries, kind, cut
        ),
        (*states, weights, gains, offsets, *totals, *extra),
        outs,
        [pltpu.VMEM((len(states) * samples, entries + 2 * width, 3 * channels), jnp.bfloat16)]
        + ([pltpu.VMEM((samples, entries, channels), jnp.float32)] if kind == "last" else []),
        flops=2 * len(states) * samples * entries * 9 * channels * channels,
        moved=4 * len(states) * samples * entries * channels,
    )


def weight_parts(inner):
    half, cut = inner // 2, inner // 2 * 5 // 8 // 16 * 16
    return half, ((0, cut), (cut, half))


def widen_kernel(part, stored, weights, *refs):
    out = refs[-3] if stored else refs[-1]
    half, parts = weight_parts(weights.shape[2])
    low, high = parts[part]
    piece = high - low
    at = pl.multiple_of((lax.axis_index("batch") % 2) * half + low, 16)
    if stored:
        held, done = refs[-2:]
        copy = pltpu.make_async_copy(weights.at[0, :, pl.ds(at, piece)], held, done)
        copy.start()
        copy.wait()
    for row in range(3):
        values = held[row] if stored else weights[0, row, pl.ds(at, piece)]
        out[row * piece : (row + 1) * piece] = values.astype(jnp.float32)


def widen(part, weights, after, stored):
    inner, channels = weights.shape[2:]
    low, high = weight_parts(inner)[1][part]
    piece = high - low
    return call(
        functools.partial(widen_kernel, part, stored),
        (weights, after),
        f32(3 * piece, channels),
        [pltpu.VMEM((3, piece, channels), jnp.bfloat16), pltpu.SemaphoreType.DMA] if stored else [],
        specs=[in_place if stored else whole, whole],
        moved=3 * piece * channels * 6,
        limit=51 << 20 if stored else vmem_bytes,
    )


def stage_kernel(first, weights, *refs):
    out, done = refs[-2:]
    copies = [
        pltpu.make_async_copy(weights.at[first + n], out.at[n], done.at[n])
        for n in range(out.shape[0])
    ]
    for copy in copies:
        copy.start()
    for copy in copies:
        copy.wait()


def stage(first, count, weights, after, limit):
    return call(
        functools.partial(stage_kernel, first),
        (weights, after),
        jax.ShapeDtypeStruct((count, *weights.shape[1:]), weights.dtype),
        [pltpu.SemaphoreType.DMA((count,))],
        specs=[in_place, whole],
        moved=weights.size,
        limit=limit,
    )


def gather_kernel(weights, near_upper, near_lower, far_upper, far_lower, out):
    parity, core = lax.axis_index("depth") % 2, lax.axis_index("batch") % 2
    out[parity] = weights[0]
    half, parts = weight_parts(weights.shape[2])
    for (low, high), pieces in zip(parts, ((near_upper, far_upper), (near_lower, far_lower))):
        for owner, source in ((core, pieces[0]), (1 - core, pieces[1])):
            at = pl.multiple_of(owner * half + low, 16)
            for row in range(3):
                values = source[row * (high - low) : (row + 1) * (high - low)]
                out[1 - parity, row, pl.ds(at, high - low)] = values.astype(jnp.bfloat16)


def relay_kernel(low, high, received, early, out):
    half, rows, width, channels = out.shape
    entries = rows * width
    odd = lax.axis_index("depth") % 2 == 1
    for i in range(half):
        passed = received[i * entries : (i + 1) * entries].reshape(rows, width, channels)
        out[i] = jnp.where(odd, early[half + i, low:high], passed)


def pair_kernel(turn, piece, cuts, start_cuts, kept, out_cuts, last, *refs):
    refs, taps = list(refs[:-1]), refs[-1]
    take = lambda count: [refs.pop(0) for _ in range(count)]
    pieces = len(cuts) + 1
    is_last = piece is None or piece == pieces - 1
    if piece is None:
        incoming, halo = take(pieces), []
    elif piece == 0:
        incoming, halo = take(1), []
    else:
        incoming, halo = take(2), take(1)
    exchange = take(pieces if piece is None else piece + 1)
    forcing, terms, kernels = take(3)
    take(1 + len(kept))
    gives = {low_high: ref for low_high, ref in zip(kept, refs[len(refs) - len(kept) :])}
    own = refs[len(refs) - len(kept) - 1]
    made = refs[: len(refs) - len(kept) - 1]
    half, height, width, channels = own.shape
    position = lax.axis_index("depth")
    parity = position % 2

    def flat(values):
        return values.reshape(-1, channels)

    def joined(values):
        return values[0] if len(values) == 1 else jnp.concatenate(values, axis=0)

    def forced(stage, i, low, high):
        here = forcing[i, low * width : high * width]
        there = []
        for (first, end), ref in zip(spans(start_cuts, height), exchange):
            a, b = max(low, first), min(high, end)
            if a < b:
                base = i * (end - first) - first
                there.append(ref[(base + a) * width : (base + b) * width])
        return jnp.where(parity == stage, here, joined(there))

    def mapped(stage, i, values, begin, low, high):
        base = half * start_cuts[0] * width
        center, scale, offset = (
            jnp.where(parity == stage, terms[n : n + 1], exchange[0][base + n : base + n + 1])
            for n in range(3)
        )
        lay_out(
            jnp.maximum((values - center) * scale + offset, 0.0),
            taps.at[i, stage],
            width,
            low == 0,
            high == height,
        )
        change = convolved(
            taps.at[i, stage], lambda row: kernels[stage, row], width, (high - low) * width
        )
        kept_values = values[(low - begin) * width : (high - begin) * width]
        return kept_values + coarse_step * change + forced(stage, i, low, high)

    def put(i, low, values, is_own):
        high = low + values.shape[0] // width
        values = values.reshape(high - low, width, channels)
        if is_own:
            own[i, low:high] = values
            return
        for (first, end), ref in gives.items():
            a, b = max(low, first), min(high, end)
            if a < b:
                ref[i, a - first : b - first] = values[a - low : b - low]

    @pl.when(position // 2 == turn)
    def _():
        for i in range(half):
            if halo:
                cut = cuts[piece - 1]
                low = (cut - 1, cut - 2)
                values = joined([flat(incoming[0][i, -2:]), flat(incoming[1][i])])
                begin = (cut - 2, cut - 3)
            else:
                low, begin = (0, 0), (0, 0)
                values = joined([flat(part[i]) for part in incoming])
            high = (height, height) if is_last else (cuts[piece] - 1, cuts[piece] - 2)
            first = mapped(0, i, values, begin[0], low[0], high[0])
            values = joined([flat(halo[0][i, -2:]), first]) if halo else first
            second = mapped(1, i, values, begin[1], low[1], high[1])
            outs = list(made)
            if not is_last:
                outs.pop(0)[i] = first.reshape(-1, width, channels)
            if not last:
                for a, b in spans(out_cuts, height) if piece is None else [(low[1], high[1])]:
                    at = slice((a - low[1]) * width, (b - low[1]) * width)
                    outs.pop(0)[i] = second[at].reshape(-1, width, channels)

            @pl.when(parity == 0)
            def _():
                put(i, low[0], first, True)
                put(i, low[1], second, False)

            @pl.when(parity == 1)
            def _():
                put(i, low[0], first, False)
                put(i, low[1], second, True)


def pair(turn, piece, cuts, start_cuts, out_cuts, last, incoming, exchange, shared, own, gives):
    half, height, width, channels = own.shape
    pieces = len(cuts) + 1
    is_last = piece is None or piece == pieces - 1
    rows = lambda low, high: f32(half, high - low, width, channels)
    made = []
    if not is_last:
        low = cuts[piece - 1] - 1 if piece else 0
        made.append(rows(low, cuts[piece] - 1))
    if not last:
        if piece is None:
            made += [rows(*span) for span in spans(out_cuts, height)]
        else:
            made.append(rows(*spans(out_cuts, height)[piece]))
    kept = tuple(gives)
    carried = (own, *gives.values())
    operands = (*incoming, *exchange, *shared, *carried)
    count = len(operands) - len(carried)
    entries = half * height * width // pieces
    outs = call(
        functools.partial(pair_kernel, turn, piece, cuts, start_cuts, kept, out_cuts, last),
        operands,
        tuple(made) + tuple(f32(*part.shape) for part in carried),
        [pltpu.VMEM((half, 2, (height + 2) * width, 3 * channels), jnp.bfloat16)],
        aliases={count + n: len(made) + n for n in range(len(carried))},
        flops=4 * entries * 9 * channels * channels,
        moved=8 * entries * channels,
    )
    rest = outs[len(made) :]
    return outs[: len(made)], rest[0], dict(zip(kept, rest[1:]))


def finish_own_kernel(early, own, own_other, out, done):
    half = own.shape[0]
    position = lax.axis_index("depth")
    here = out.at[pl.ds((position % 2) * half, half)]
    for condition, source, target in (
        (position < 2, early, out),
        ((position >= 2) & (position // 2 % 2 == 0), own, here),
        (position // 2 % 2 == 1, own_other, here),
    ):

        @pl.when(condition)
        def _(source=source, target=target):
            copy = pltpu.make_async_copy(source, target, done)
            copy.start()
            copy.wait()


def finish_kernel(cuts, *refs):
    pieces, out, done = refs[: len(cuts) + 1], refs[-2], refs[-1]
    half = pieces[0].shape[0]
    position = lax.axis_index("depth")

    @pl.when(position >= 2)
    def _():
        there = pl.ds((1 - position % 2) * half, half)
        copies = [
            pltpu.make_async_copy(piece, out.at[there, low:high], done.at[n])
            for n, (piece, (low, high)) in enumerate(zip(pieces, spans(cuts, out.shape[1])))
        ]
        for copy in copies:
            copy.start()
        for copy in copies:
            copy.wait()


def turns_of(count, height):
    start = (height // 2, height * 7 // 8)
    plan, cuts = [], start
    for _ in range(count):
        split = cuts[0] >= 3
        plan.append((cuts, split, tuple(cut - 2 for cut in cuts) if split else start))
        cuts = plan[-1][2]
    return start, plan


def steps(iterate, weights, norm_scale, norm_shift):
    initial = iterate[0]
    samples, rows, width, channels = initial.shape
    half = samples // 2
    devices = lax.axis_size("depth")
    group = lax.axis_size("batch")
    batch_entries = samples * rows * width * group
    weights = weights.reshape(layers_of_block, 3, 3 * channels, channels)
    run = functools.partial(layer, batch_entries=batch_entries)

    def gathered(sums, mark=False, chips=False, ready=()):
        others = [
            lax.ppermute(sums, "batch", [(i, i ^ m) for i in range(group)])
            for m in (range(3, group, 2) if chips else range(1, group))
        ]
        if mark:
            sums = call(copy_kernel, (sums, *ready), f32(*sums.shape))
        return (sums, *others)

    both = ("depth", "batch")

    def routes(of):
        return [
            (i * group + b, of(i)[0] * group + (b ^ 1 if of(i)[1] else b))
            for i in range(devices)
            for b in range(group)
        ]

    swaps = routes(lambda i: (i ^ 1, i // 2 % 2 == 1))
    backs = routes(lambda i: (i ^ 1, i // 2 % 2 == 1) if i > 1 else (i, True))
    partners = [(i, i ^ 1) for i in range(devices)]
    cores = [(i, i ^ 1) for i in range(group)]
    onward = [(i, i + 1) for i in range(devices - 1)]

    initial, sums = call(
        sums_kernel, (initial,), (f32(*initial.shape), f32(2, channels)), moved=initial.size * 4
    )
    first_totals = gathered(sums)
    other = lax.ppermute(initial, "batch", cores)
    near_upper = lax.ppermute(widen(0, weights, sums, True), "depth", partners)
    head = stage(0, 1, weights, sums, 51 << 20)
    norms = (norm_scale, norm_shift)
    states, totals = (initial, other), first_totals
    for number in range(layers_of_block - 1):
        keep = 2 if number < layers_of_block - 2 else 1
        if number == 0:
            *states, sums = run(0, states, (head,), *norms, totals, kind="plain", keep=keep)
            rest = stage(1, layers_of_block - 1, weights, sums, 48 << 20)
            norms = ((head, rest), *norms)
        else:
            *states, sums = run(number, states, *norms, totals, kind="plain", keep=keep)
        totals = gathered(sums, False, True)
    current, sums = run(layers_of_block - 1, states[:1], *norms, totals, kind="plain")
    totals = gathered(sums)
    arrived = lax.ppermute(current, "depth", onward)
    arrived_totals = lax.ppermute(sum(totals[1:], totals[0]), "depth", onward)

    start, plan = turns_of(devices // 2 - 1, rows)
    current, sums, coarse_begin, terms = run(
        0, (arrived,), *norms, (arrived_totals,), kind="first", extra=(initial, *first_totals)
    )
    other = lax.ppermute(current, "batch", cores)
    near_lower = lax.ppermute(widen(1, head, sums, False), "depth", partners)
    far_upper = lax.ppermute(near_upper, "batch", cores)
    states = (current, other)
    for number in range(1, layers_of_block - 1):
        totals = gathered(sums, number == 1, number > 1)
        keep = 2 if number < layers_of_block - 2 else 1
        *states, sums = run(number, states, *norms, totals, kind="plain", keep=keep)
    far_lower = lax.ppermute(near_lower, "batch", cores)
    early, mine, *sent = run(
        layers_of_block - 1,
        states[:1],
        *norms,
        gathered(sums, True, True),
        kind="last",
        extra=(coarse_begin, terms),
        cut=start,
    )
    kernels = call(
        gather_kernel,
        (head, near_upper, near_lower, far_upper, far_lower),
        jax.ShapeDtypeStruct((2, 3, 3 * channels, channels), jnp.bfloat16),
        moved=9 * channels * channels * 8,
    )

    exchange = [lax.ppermute(part, both, swaps) for part in sent]
    mine_other = lax.ppermute(mine, "batch", cores)
    passed = [
        call(
            functools.partial(relay_kernel, low, high),
            (part, early),
            f32(half, high - low, width, channels),
            moved=half * (high - low) * width * channels * 8,
        )
        for part, (low, high) in zip(exchange, spans(start, rows))
    ]
    own = jnp.zeros((half, rows, width, channels), jnp.float32)
    gives = {
        (low, high): jnp.zeros((half, high - low, width, channels), jnp.float32)
        for low, high in spans(plan[-1][2], rows)
    }
    back_spans = list(gives)
    back = []
    for turn, (cuts, split, out_cuts) in enumerate(plan, 1):
        across = {}
        for i in (2 * turn - 2, 2 * turn - 1):
            across[i], across[i + 2] = i + 2, i
        route = routes(lambda i: (across.get(i, i), True))
        arriving = [lax.ppermute(part, both, route) for part in passed]
        shared = (mine_other if turn % 2 else mine, terms, kernels)
        last = turn == len(plan)
        if not split:
            passed, own, gives = pair(
                turn, None, cuts, start, out_cuts, last, arriving, exchange, shared, own, gives
            )
            continue
        passed, halo = [], ()
        for n in range(len(cuts) + 1):
            incoming = (*arriving[max(n - 1, 0) : n + 1], *halo)
            now = {span: gives[span] for span in back_spans[n : n + 2]} if last else gives
            made, own, now = pair(
                turn,
                n,
                cuts,
                start,
                out_cuts,
                last,
                incoming,
                exchange[: n + 1],
                shared,
                own,
                now,
            )
            gives = {**gives, **now}
            halo = tuple(made[:1]) if n < len(cuts) else ()
            if last:
                back.append(lax.ppermute(gives[back_spans[n]], both, backs))
            else:
                passed.append(made[-1])
    if not back:
        back = [lax.ppermute(part, both, backs) for part in gives.values()]
    out = call(
        finish_own_kernel,
        (early, own, lax.ppermute(own, "batch", cores)),
        f32(*initial.shape),
        [pltpu.SemaphoreType.DMA],
        out_specs=in_place,
        moved=initial.size * 8,
    )
    out = call(
        functools.partial(finish_kernel, plan[-1][2]),
        (*back, out),
        f32(*initial.shape),
        [pltpu.SemaphoreType.DMA((len(back),))],
        specs=[whole] * len(back) + [in_place],
        out_specs=in_place,
        aliases={len(back): 0},
        moved=initial.size * 4,
    )
    return out[None]


def solution(mesh):
    return jax.shard_map(
        steps,
        mesh=mesh,
        in_specs=(
            P("depth", "batch", None, None, None),
            P("depth", None, None, None, None),
            P("depth", None),
            P("depth", None),
        ),
        out_specs=P("depth", "batch", None, None, None),
        check_vma=False,
    )
```
